128 devices in a mesh: pipe: 8 (over x, z_hi), tensor: 16 (over z_lo, y, core).
Axes of the slice: x: 4, y: 4, z: 4 (z_hi: 2, z_lo: 2; z = z_hi * 2 + z_lo), core: 2. Of those that a mesh axis runs over, the one named last changes fastest.
Arguments:
- layer_input: bfloat16 [768, 8192], P('tensor', 'pipe'), may hold values from -6 to 6
- out_grad: bfloat16 [768, 8192], P('tensor', 'pipe'), may hold values from -2 to 2
- gate_pre: bfloat16 [768, 28672], P(None, 'tensor'), may hold values from -8 to 8
- up_pre: bfloat16 [768, 28672], P(None, 'tensor'), may hold values from -6 to 6
- gate_weight: bfloat16 [8192, 28672], P('pipe', 'tensor'), may hold values from -0.0625 to 0.0625
- up_weight: bfloat16 [8192, 28672], P('pipe', 'tensor'), may hold values from -0.0625 to 0.0625
- down_weight: bfloat16 [28672, 8192], P('tensor', 'pipe'), may hold values from -0.03125 to 0.03125
- gate_mask: int32 [64, 224], P('pipe', 'tensor'), may hold values from 0 to 1, as said below
- up_mask: int32 [64, 224], P('pipe', 'tensor'), may hold values from 0 to 1, as said below
- down_mask: int32 [224, 64], P('tensor', 'pipe'), may hold values from 0 to 1, as said below
Outputs:
- grad_input: bfloat16 [768, 8192], P('tensor', 'pipe')
- grad_gate: bfloat16 [8192, 28672], P('pipe', 'tensor')
- grad_up: bfloat16 [8192, 28672], P('pipe', 'tensor')
- grad_down: bfloat16 [28672, 8192], P('tensor', 'pipe')
The draws below stay inside these ranges and needn't reach their ends.
Inputs may be any that keep to these rules, and one draw needn't show every extreme that they name: `gate_mask`: each entry is 1 for a kept block and 0 for a pruned one; the share of kept blocks differs from block column to block column. `up_mask`: each entry is 1 for a kept block and 0 for a pruned one; the share of kept blocks differs from block column to block column. `down_mask`: each entry is 1 for a kept block and 0 for a pruned one; the share of kept blocks differs from block row to block row.
All inputs are finite; a program needn't handle non-finite values.
Results may differ from the reference program's by a relative error of at most 0.005.
Values may be sent and summed in bfloat16 or wider, within the bound.
A program may use at most 128 MiB of HBM per device.

```python
import jax
import jax.numpy as jnp
from jax import lax

D = 8192
FF = 28672
BLOCK = 128
TOKENS = 768


def block_mask(key, rows, cols, by_rows):
    level_key, value_key = jax.random.split(key)
    if by_rows:
        level = jax.random.randint(level_key, (rows, 1), 1, 8)
    else:
        level = jax.random.randint(level_key, (1, cols), 1, 8)
    values = jax.random.randint(value_key, (rows, cols), 0, 8)
    return (values < level).astype(jnp.int32)


def draw_gate_mask(key, part):
    return block_mask(jax.random.fold_in(key, 11), D // BLOCK, FF // BLOCK, False)


def draw_up_mask(key, part):
    return block_mask(jax.random.fold_in(key, 23), D // BLOCK, FF // BLOCK, False)


def draw_down_mask(key, part):
    return block_mask(jax.random.fold_in(key, 37), FF // BLOCK, D // BLOCK, True)


def steps_of(stream_key, shape, cuts, low, largest):
    def one(position, shards_of):
        steps = jax.random.uniform(jax.random.fold_in(jax.random.fold_in(stream_key, 6), position), (shards_of,), jnp.float32, low / len(cuts), largest / len(cuts))
        return jnp.repeat(jnp.exp(steps), shape[position] // shards_of).reshape((-1,) + (1,) * (len(shape) - position - 1))

    factor_of = one(*cuts[0])
    for cut in cuts[1:]:
        factor_of = factor_of * one(*cut)
    return factor_of


def normal_values(rng, extent, scale, bound, cuts=(), kind=jnp.bfloat16):
    values = scale * jax.random.normal(rng, extent, jnp.float32)
    if cuts:
        values = values * steps_of(rng, extent, cuts, -0.22, 0.18)
    return jnp.clip(values, -bound, bound).astype(kind)


def setup_inputs(seed: int = 0) -> dict:
    keys = jax.random.split(jax.random.key(seed), 11)
    return {
        "layer_input": normal_values(keys[0], (TOKENS, D), 1.0, 6.0, ((0, 16), (1, 8))),
        "out_grad": normal_values(keys[1], (TOKENS, D), 0.25, 2.0, ((0, 16), (1, 8))),
        "gate_pre": normal_values(keys[2], (TOKENS, FF), 1.5, 8.0, ((1, 16),)),
        "up_pre": normal_values(keys[3], (TOKENS, FF), 1.0, 6.0, ((1, 16),)),
        "gate_weight": normal_values(keys[4], (D, FF), D ** -0.5, 0.0625, ((0, 8), (1, 16))),
        "up_weight": normal_values(keys[5], (D, FF), D ** -0.5, 0.0625, ((0, 8), (1, 16))),
        "down_weight": normal_values(keys[6], (FF, D), FF ** -0.5, 0.03125, ((0, 16), (1, 8))),
        "gate_mask": draw_gate_mask(jax.random.fold_in(keys[10], 71), 0),
        "up_mask": draw_up_mask(jax.random.fold_in(keys[10], 71), 0),
        "down_mask": draw_down_mask(jax.random.fold_in(keys[10], 71), 0),
    }


def expand(mask):
    return jnp.repeat(jnp.repeat(mask, BLOCK, axis=0), BLOCK, axis=1)


def reference(layer_input, out_grad, gate_pre, up_pre, gate_weight, up_weight, down_weight, gate_mask, up_mask, down_mask):
    slab_count = 16
    width = FF // slab_count
    nblocks = width // BLOCK

    def split_cols(array, per):
        return array.reshape(array.shape[0], slab_count, per).transpose(1, 0, 2)

    items = (split_cols(gate_weight, width), split_cols(up_weight, width), down_weight.reshape(slab_count, width, D),
             split_cols(gate_mask, nblocks), split_cols(up_mask, nblocks), down_mask.reshape(slab_count, nblocks, D // BLOCK),
             split_cols(gate_pre, width), split_cols(up_pre, width))

    def one_slab(carry, slab):
        wg_s, wu_s, wd_s, mg_s, mu_s, md_s, gp_s, up_s = slab
        mask_gate = expand(mg_s)
        mask_up = expand(mu_s)
        mask_down = expand(md_s)
        gate_masked = wg_s * mask_gate.astype(jnp.bfloat16)
        up_masked = wu_s * mask_up.astype(jnp.bfloat16)
        down_masked = wd_s * mask_down.astype(jnp.bfloat16)
        hidden_grad = jnp.dot(out_grad, down_masked.T, preferred_element_type=jnp.float32)
        gate_val = gp_s.astype(jnp.float32)
        up_val = up_s.astype(jnp.float32)
        sigma_val = jax.nn.sigmoid(gate_val)
        hidden = (gate_val * sigma_val * up_val).astype(jnp.bfloat16)
        grad_down = (jnp.dot(hidden.T, out_grad, preferred_element_type=jnp.float32) * mask_down.astype(jnp.float32)).astype(jnp.bfloat16)
        gate_grad = (hidden_grad * up_val * sigma_val * (1.0 + gate_val * (1.0 - sigma_val))).astype(jnp.bfloat16)
        up_grad = (hidden_grad * gate_val * sigma_val).astype(jnp.bfloat16)
        grad_gate = (jnp.dot(layer_input.T, gate_grad, preferred_element_type=jnp.float32) * mask_gate.astype(jnp.float32)).astype(jnp.bfloat16)
        grad_up = (jnp.dot(layer_input.T, up_grad, preferred_element_type=jnp.float32) * mask_up.astype(jnp.float32)).astype(jnp.bfloat16)
        carry = carry + jnp.dot(gate_grad, gate_masked.T, preferred_element_type=jnp.float32)
        carry = carry + jnp.dot(up_grad, up_masked.T, preferred_element_type=jnp.float32)
        return carry, (grad_gate, grad_up, grad_down)

    total, (grad_gate, grad_up, grad_down) = lax.scan(one_slab, jnp.zeros((TOKENS, D), jnp.float32), items)
    grad_gate = grad_gate.transpose(1, 0, 2).reshape(D, FF)
    grad_up = grad_up.transpose(1, 0, 2).reshape(D, FF)
    grad_down = grad_down.reshape(FF, D)
    return (total.astype(jnp.bfloat16), grad_gate, grad_up, grad_down)
```

```python
import jax
import jax.numpy as jnp
from jax import lax
from jax.experimental import pallas as pl
from jax.experimental.pallas import tpu as pltpu
from jax.sharding import PartitionSpec as P

MESH = pl.DeviceIdType.MESH
BF = jnp.bfloat16
F32 = jnp.float32
ROWS = 48
D = 1024
FF = 1792
NA = 8
NC = 14
GATHER = 15


def coords():
    p, t = lax.axis_index("pipe"), lax.axis_index("tensor")
    return (
        lax.div(p, 2),
        lax.rem(p, 2),
        lax.div(t, 8),
        lax.rem(lax.div(t, 2), 4),
        lax.rem(t, 2),
    )


def device(x, zh, zl, y, c):
    return (lax.rem(x, 4) * 2 + zh, zl * 8 + lax.rem(y, 4) * 2 + c)


def rank(zl, y, c):
    return zl * 8 + lax.rem(y, 4) * 2 + c


class Copies:
    def __init__(self, send, recv):
        self.send, self.recv, self.all = send, recv, []

    def start(self, i, src, dst, dev):
        c = pltpu.make_async_remote_copy(
            src_ref=src,
            dst_ref=dst,
            send_sem=self.send.at[i],
            recv_sem=self.recv.at[i],
            device_id=dev,
            device_id_type=MESH,
        )
        c.start()
        self.all.append(c)
        return c

    def finish(self):
        for c in self.all:
            c.wait_send()


class Gather:
    def __init__(self, cp, base, src, full, sem):
        self.cp, self.base, self.full = cp, base, full
        x, zh, zl, y, c = self.at = coords()
        me = rank(zl, y, c)
        self.own = pltpu.make_async_copy(src, full.at[me], sem)
        self.own.start()
        dst = full.at[me]
        self.z = cp.start(base, src, dst, device(x, zh, 1 - zl, y, c))
        self.y1 = [cp.start(base + k, src, dst, device(x, zh, zl, y + k, c)) for k in (1, 3, 2)]
        self.sib = [cp.start(base + 7, src, dst, device(x, zh, zl, y, 1 - c))]
        self.n = 7

    def to_sibling(self, r):
        x, zh, zl, y, c = self.at
        self.n += 1
        piece = self.full.at[r]
        self.sib.append(self.cp.start(self.base + self.n, piece, piece, device(x, zh, zl, y, 1 - c)))

    def step_z(self):
        x, zh, zl, y, c = self.at
        self.z.wait_recv()
        piece = self.full.at[rank(1 - zl, y, c)]
        self.y2 = [
            self.cp.start(self.base + 3 + k, piece, piece, device(x, zh, zl, y + k, c))
            for k in (1, 3, 2)
        ]
        self.to_sibling(rank(1 - zl, y, c))

    def step_y(self):
        x, zh, zl, y, c = self.at
        for copies, z in ((self.y1, zl), (self.y2, 1 - zl)):
            for copy, k in zip(copies, (1, 3, 2)):
                copy.wait_recv()
                self.to_sibling(rank(z, y + 4 - k, c))

    def finish(self):
        for copy in self.sib:
            copy.wait_recv()
        self.own.wait()


def add(*refs):
    total = refs[0][...].astype(F32)
    for r in refs[1:]:
        total = total + r[...].astype(F32)
    return total


def hidden_kernel(
    mask_ref, x_hbm, og_hbm, dw_hbm,
    hg, x_full, og_full,
    dw, hp, rl1, rl2, rl3, rr1, rr2, rr3, asum, fa, rz,
    rb, bs, bl1, bl2, bl3, br1, br2, br3,
    send, recv, local,
):
    x, zh, zl, y, c = coords()
    right, left = device(x + 1, zh, zl, y, c), device(x + 3, zh, zl, y, c)
    other = device(x, 1 - zh, zl, y, c)
    x1, x2, x3 = lax.rem(x + 1, 4), lax.rem(x + 2, 4), lax.rem(x + 3, 4)

    barrier = pltpu.get_barrier_semaphore()
    partners = [right, left, other, device(x, zh, 1 - zl, y, c), device(x, zh, zl, y, 1 - c)]
    partners += [device(x, zh, zl, y + k, c) for k in (1, 2, 3)]
    load = pltpu.make_async_copy(dw_hbm, dw, local.at[0])
    load.start()
    for d in partners:
        pl.semaphore_signal(barrier, inc=1, device_id=d, device_id_type=MESH)
    pl.semaphore_wait(barrier, len(partners))

    cp = Copies(send, recv)
    og = Gather(cp, 0, og_hbm, og_full, local.at[1])
    load.wait()

    @pl.loop(0, NC)
    def _(i):
        for k in range(D // 128):
            at = (pl.ds(pl.multiple_of(i * 128, 128), 128), pl.ds(k * 128, 128))
            dw[at] = dw[at] * mask_ref[i, k].astype(F32).astype(BF)

    og.step_z()
    og.step_y()
    og.finish()

    def partial(first, last):
        @pl.loop(first // 2, last // 2)
        def _(j):
            w = dw[pl.ds(pl.multiple_of(j * 256, 256), 256), :]
            acc = lax.dot_general(
                og_full[...].reshape(768, D), w, (((1,), (1,)), ((), ())), preferred_element_type=F32
            ).astype(BF)
            hp[2 * j] = acc[:, :128].reshape(2, 4, 96, 128)
            hp[2 * j + 1] = acc[:, 128:].reshape(2, 4, 96, 128)

    L, R, B = pl.ds(0, 4), pl.ds(4, 4), pl.ds(NA, 6)
    BL, BR = pl.ds(0, 3), pl.ds(3, 3)
    s = 2 * GATHER
    partial(NA, NC)
    zb = cp.start(s, hp.at[B, 1 - zh], rb, other)
    partial(0, 4)
    a1r = cp.start(s + 1, hp.at[L, :, x2], rl1, right)
    partial(4, 8)
    a1l = cp.start(s + 2, hp.at[R, :, x2], rr1, left)
    a2r = cp.start(s + 3, hp.at[R, :, x1], rl2, right)
    a2l = cp.start(s + 4, hp.at[L, :, x3], rr2, left)
    inp = Gather(cp, GATHER, x_hbm, x_full, local.at[2])
    a1r.wait_recv()
    rl1[...] = add(rl1, hp.at[L, :, x1]).astype(BF)
    a3r = cp.start(s + 5, rl1, rl3, right)
    a1l.wait_recv()
    rr1[...] = add(rr1, hp.at[R, :, x3]).astype(BF)
    a3l = cp.start(s + 6, rr1, rr3, left)
    inp.step_z()
    zb.wait_recv()
    bs[...] = add(rb, hp.at[B, zh]).astype(BF)
    b1r = cp.start(s + 8, bs.at[BL, x2], bl1, right)
    b1l = cp.start(s + 9, bs.at[BR, x2], br1, left)
    b2r = cp.start(s + 10, bs.at[BR, x1], bl2, right)
    b2l = cp.start(s + 11, bs.at[BL, x3], br2, left)
    inp.step_y()
    for copy in (a2r, a2l, a3r, a3l):
        copy.wait_recv()
    asum[L] = add(hp.at[L, :, x], rl3, rr2)
    asum[R] = add(hp.at[R, :, x], rr3, rl2)
    fa[...] = asum[:, 1 - zh].astype(BF)
    za = cp.start(s + 7, fa, rz, other)
    b1r.wait_recv()
    bl1[...] = add(bl1, bs.at[BL, x1]).astype(BF)
    b3r = cp.start(s + 12, bl1, bl3, right)
    b1l.wait_recv()
    br1[...] = add(br1, bs.at[BR, x3]).astype(BF)
    b3l = cp.start(s + 13, br1, br3, left)
    inp.finish()

    g = s + 14
    A, AL, AR = pl.ds(0, NA), pl.ds(0, 4), pl.ds(4, 4)
    GL, GR = pl.ds(NA, 3), pl.ds(NA + 3, 3)

    def send_rows(i, cols, h, q, dev):
        piece = hg.at[cols, h, q]
        return cp.start(g + i, piece, piece, dev)

    za.wait_recv()
    hg[A, zh, x] = add(asum.at[:, zh], rz).astype(BF)
    ga = send_rows(0, A, zh, x, other)
    gr = [send_rows(1, A, zh, x, right)]
    gl = [send_rows(2, A, zh, x, left)]
    for copy in (b2r, b2l, b3r, b3l):
        copy.wait_recv()
    hg[GL, zh, x] = add(bs.at[BL, x], bl3, br2).astype(BF)
    hg[GR, zh, x] = add(bs.at[BR, x], br3, bl2).astype(BF)
    br = send_rows(9, B, zh, x, right)
    bl = send_rows(10, B, zh, x, left)
    z = [send_rows(13, B, zh, x, other)]
    ga.wait_recv()
    gr.append(send_rows(3, A, 1 - zh, x, right))
    gl.append(send_rows(4, A, 1 - zh, x, left))
    br.wait_recv()
    fr = send_rows(11, GL, zh, x3, right)
    z.append(send_rows(14, B, zh, x3, other))
    bl.wait_recv()
    fl = send_rows(12, GR, zh, x1, left)
    z.append(send_rows(15, B, zh, x1, other))
    f = []
    gr[0].wait_recv()
    f.append(send_rows(5, AL, zh, x3, right))
    gl[0].wait_recv()
    f.append(send_rows(6, AR, zh, x1, left))
    fr.wait_recv()
    z.append(send_rows(16, GL, zh, x2, other))
    fl.wait_recv()
    z.append(send_rows(17, GR, zh, x2, other))
    gr[1].wait_recv()
    f.append(send_rows(7, AL, 1 - zh, x3, right))
    gl[1].wait_recv()
    f.append(send_rows(8, AR, 1 - zh, x1, left))
    for copy in f + z:
        copy.wait_recv()
    cp.finish()


def hidden_gradient(down_mask, layer_input, out_grad, down_weight):
    vmem = pl.BlockSpec(memory_space=pltpu.VMEM)
    hbm = pl.BlockSpec(memory_space=pl.ANY)
    a = pltpu.VMEM((4, 2, 96, 128), BF)
    b = pltpu.VMEM((3, 96, 128), BF)
    copies = 2 * GATHER + 14 + 18
    return pl.pallas_call(
        hidden_kernel,
        name="hidden_gradient",
        out_shape=(
            jax.ShapeDtypeStruct((NC, 2, 4, 96, 128), BF),
            jax.ShapeDtypeStruct((16, ROWS, D), BF),
            jax.ShapeDtypeStruct((16, ROWS, D), BF),
        ),
        in_specs=[pl.BlockSpec(memory_space=pltpu.SMEM), hbm, hbm, hbm],
        out_specs=(vmem, vmem, vmem),
        scratch_shapes=[
            pltpu.VMEM((FF, D), BF),
            pltpu.VMEM((NC, 2, 4, 96, 128), BF),
            a, a, a, a, a, a,
            pltpu.VMEM((NA, 2, 96, 128), F32),
            pltpu.VMEM((NA, 96, 128), BF),
            pltpu.VMEM((NA, 96, 128), BF),
            pltpu.VMEM((6, 4, 96, 128), BF),
            pltpu.VMEM((6, 4, 96, 128), BF),
            b, b, b, b, b, b,
            pltpu.SemaphoreType.DMA((copies,)),
            pltpu.SemaphoreType.DMA((copies,)),
            pltpu.SemaphoreType.DMA((3,)),
        ],
        compiler_params=pltpu.CompilerParams(
            collective_id=0, has_side_effects=True, vmem_limit_bytes=56 * 1024 * 1024
        ),
    )(down_mask, layer_input, out_grad, down_weight)


def grads_kernel(
    gm, um, dm, hg, gp, up, x_ref, og_ref, gw, uw,
    total, g_gate, g_up, g_down,
    xt,
):
    j = pl.program_id(0)

    @pl.when(j == 0)
    def _():
        xt[...] = x_ref[...].T
        total[...] = jnp.zeros_like(total)

    grad = jnp.concatenate([hg[0], hg[1]], axis=1).astype(F32)
    gate, upv = gp[...].astype(F32), up[...].astype(F32)
    s = jax.nn.sigmoid(gate)
    gs = gate * s
    hidden = (gs * upv).astype(BF)
    gate_grad = (grad * upv * s * (1.0 + gate * (1.0 - s))).astype(BF)
    up_grad = (grad * gs).astype(BF)

    def weight_grad(lhs, rhs, out, mask):
        acc = jnp.dot(lhs, rhs, preferred_element_type=F32)
        for a in range(acc.shape[0] // 128):
            for b in range(acc.shape[1] // 128):
                at = (slice(a * 128, a * 128 + 128), slice(b * 128, b * 128 + 128))
                out[at] = (acc[at] * mask(a, b).astype(F32)).astype(BF)

    def masked(w, mask):
        return jnp.concatenate(
            [
                jnp.concatenate(
                    [
                        w[a * 128 : a * 128 + 128, b * 128 : b * 128 + 128]
                        * mask(a, b).astype(F32).astype(BF)
                        for b in range(2)
                    ],
                    axis=1,
                )
                for a in range(D // 128)
            ],
            axis=0,
        )

    gmask = lambda a, b: gm[a, 2 * j + b]
    umask = lambda a, b: um[a, 2 * j + b]
    weight_grad(xt[...], gate_grad, g_gate, gmask)
    weight_grad(xt[...], up_grad, g_up, umask)
    weight_grad(hidden.T, og_ref[...], g_down, lambda a, b: dm[2 * j + a, b])
    nt = (((1,), (1,)), ((), ()))
    total[...] += lax.dot_general(
        gate_grad, masked(gw, gmask), nt, preferred_element_type=F32
    ) + lax.dot_general(up_grad, masked(uw, umask), nt, preferred_element_type=F32)


def grads(gate_mask, up_mask, down_mask, hg, gate_pre, up_pre, x_full, og_full, gate_weight, up_weight):
    smem = pl.BlockSpec(memory_space=pltpu.SMEM)
    cols = pl.BlockSpec((768, 256), lambda j: (0, j))
    whole = pl.BlockSpec((768, D), lambda j: (0, 0))
    weight = pl.BlockSpec((D, 256), lambda j: (0, j))
    return pl.pallas_call(
        grads_kernel,
        name="grads",
        grid=(FF // 256,),
        out_shape=(
            jax.ShapeDtypeStruct((768, D), F32),
            jax.ShapeDtypeStruct((D, FF), BF),
            jax.ShapeDtypeStruct((D, FF), BF),
            jax.ShapeDtypeStruct((FF, D), BF),
        ),
        in_specs=[
            smem, smem, smem,
            pl.BlockSpec((2, 768, 128), lambda j: (j, 0, 0)),
            cols, cols, whole, whole, weight, weight,
        ],
        out_specs=(whole, weight, weight, pl.BlockSpec((256, D), lambda j: (j, 0))),
        scratch_shapes=[pltpu.VMEM((D, 768), BF)],
        compiler_params=pltpu.CompilerParams(vmem_limit_bytes=48 * 1024 * 1024),
    )(gate_mask, up_mask, down_mask, hg, gate_pre, up_pre, x_full, og_full, gate_weight, up_weight)


def scatter_kernel(total, out, sib_out, sib_in, mine, got, send, recv):
    x, zh, zl, y, c = coords()
    sibling = device(x, zh, zl, y, 1 - c)
    peers = [
        (k, device(x, zh, lax.rem(zl + k // 4, 2), y + k % 4, c), lax.rem(zl + k // 4, 2) * 4 + lax.rem(y + k % 4, 4))
        for k in range(1, 8)
    ]
    barrier = pltpu.get_barrier_semaphore()
    for d in [sibling] + [p[1] for p in peers]:
        pl.semaphore_signal(barrier, inc=1, device_id=d, device_id_type=MESH)
    pl.semaphore_wait(barrier, 8)
    cp = Copies(send, recv)
    sib_out[...] = total[:, 1 - c].astype(BF)
    s = cp.start(0, sib_out, sib_in, sibling)
    s.wait_recv()
    mine[...] = add(total.at[:, c], sib_in).astype(BF)
    copies = [cp.start(k, mine.at[i], got.at[k], d) for k, d, i in peers]
    acc = mine[zl * 4 + y].astype(F32)
    for k, copy in zip(range(1, 8), copies):
        copy.wait_recv()
        acc = acc + got[k].astype(F32)
    out[...] = acc.astype(BF)
    cp.finish()


def scatter(total):
    vmem = pl.BlockSpec(memory_space=pltpu.VMEM)
    piece = pltpu.VMEM((8, ROWS, D), BF)
    return pl.pallas_call(
        scatter_kernel,
        name="scatter",
        out_shape=jax.ShapeDtypeStruct((ROWS, D), BF),
        in_specs=[vmem],
        out_specs=vmem,
        scratch_shapes=[
            piece, piece, piece, piece,
            pltpu.SemaphoreType.DMA((8,)),
            pltpu.SemaphoreType.DMA((8,)),
        ],
        compiler_params=pltpu.CompilerParams(
            collective_id=1, has_side_effects=True, vmem_limit_bytes=32 * 1024 * 1024
        ),
    )(total)


def shards(
    layer_input,
    out_grad,
    gate_pre,
    up_pre,
    gate_weight,
    up_weight,
    down_weight,
    gate_mask,
    up_mask,
    down_mask,
):
    hg, x_full, og_full = hidden_gradient(down_mask, layer_input, out_grad, down_weight)
    total, grad_gate, grad_up, grad_down = grads(
        gate_mask,
        up_mask,
        down_mask,
        hg.reshape(NC, 768, 128),
        gate_pre,
        up_pre,
        x_full.reshape(768, D),
        og_full.reshape(768, D),
        gate_weight,
        up_weight,
    )
    grad_input = scatter(total.reshape(8, 2, ROWS, D))
    return (grad_input, grad_gate, grad_up, grad_down)


def solution(mesh):
    in_specs = (
        P("tensor", "pipe"),
        P("tensor", "pipe"),
        P(None, "tensor"),
        P(None, "tensor"),
        P("pipe", "tensor"),
        P("pipe", "tensor"),
        P("tensor", "pipe"),
        P("pipe", "tensor"),
        P("pipe", "tensor"),
        P("tensor", "pipe"),
    )
    out_specs = (P("tensor", "pipe"), P("pipe", "tensor"), P("pipe", "tensor"), P("tensor", "pipe"))
    return jax.shard_map(shards, mesh=mesh, in_specs=in_specs, out_specs=out_specs, check_vma=False)
```

```python
import jax
import jax.numpy as jnp
from jax import lax
from jax.experimental import pallas as pl
from jax.experimental.pallas import tpu as pltpu
from jax.sharding import PartitionSpec as P

MESH = pl.DeviceIdType.MESH
BF = jnp.bfloat16
F32 = jnp.float32
ROWS = 48
D = 1024
FF = 1792
NA = 8
NC = 14
GATHER = 15
VMEM = 60 * 1024 * 1024


def coords():
    p, t = lax.axis_index("pipe"), lax.axis_index("tensor")
    return (
        lax.div(p, 2),
        lax.rem(p, 2),
        lax.div(t, 8),
        lax.rem(lax.div(t, 2), 4),
        lax.rem(t, 2),
    )


def device(x, zh, zl, y, c):
    return (lax.rem(x, 4) * 2 + zh, zl * 8 + lax.rem(y, 4) * 2 + c)


def rank(zl, y, c):
    return zl * 8 + lax.rem(y, 4) * 2 + c


class Copies:
    def __init__(self, send, recv):
        self.send, self.recv, self.all = send, recv, []

    def start(self, i, src, dst, dev):
        c = pltpu.make_async_remote_copy(
            src_ref=src,
            dst_ref=dst,
            send_sem=self.send.at[i],
            recv_sem=self.recv.at[i],
            device_id=dev,
            device_id_type=MESH,
        )
        c.start()
        self.all.append(c)
        return c

    def finish(self):
        for c in self.all:
            c.wait_send()


class Gather:
    def __init__(self, cp, base, src, full, sem):
        self.cp, self.base, self.full, self.src = cp, base, full, src
        x, zh, zl, y, c = self.at = coords()
        self.me = full.at[rank(zl, y, c)]
        self.own = pltpu.make_async_copy(src, self.me, sem)
        self.own.start()
        self.z = cp.start(base, src, self.me, device(x, zh, 1 - zl, y, c))
        self.n = 7

    def start_y(self):
        x, zh, zl, y, c = self.at
        self.y1 = [
            self.cp.start(self.base + k, self.src, self.me, device(x, zh, zl, y + k, c)) for k in (1, 3, 2)
        ]
        self.sib = [self.cp.start(self.base + 7, self.src, self.me, device(x, zh, zl, y, 1 - c))]

    def to_sibling(self, r):
        x, zh, zl, y, c = self.at
        self.n += 1
        piece = self.full.at[r]
        self.sib.append(self.cp.start(self.base + self.n, piece, piece, device(x, zh, zl, y, 1 - c)))

    def step_z(self):
        x, zh, zl, y, c = self.at
        self.z.wait_recv()
        piece = self.full.at[rank(1 - zl, y, c)]
        self.y2 = [
            self.cp.start(self.base + 3 + k, piece, piece, device(x, zh, zl, y + k, c)) for k in (1, 3, 2)
        ]
        self.to_sibling(rank(1 - zl, y, c))

    def step_y(self):
        x, zh, zl, y, c = self.at
        for copies, z in ((self.y1, zl), (self.y2, 1 - zl)):
            for copy, k in zip(copies, (1, 3, 2)):
                copy.wait_recv()
                self.to_sibling(rank(z, y + 4 - k, c))

    def finish(self):
        for copy in self.sib:
            copy.wait_recv()
        self.own.wait()


def add(*refs):
    total = refs[0][...].astype(F32)
    for r in refs[1:]:
        total = total + r[...].astype(F32)
    return total


def mask_columns(w, mask_ref):
    @pl.loop(0, NC)
    def _(j):
        for k in range(D // 128):
            at = (pl.ds(k * 128, 128), pl.ds(pl.multiple_of(j * 128, 128), 128))
            w[at] = w[at] * mask_ref[k, j].astype(F32).astype(BF)


NT = (((1,), (1,)), ((), ()))


def main_kernel(
    dm, gm, um, x_hbm, og_hbm, gp_hbm, up_hbm, gw_hbm, uw_hbm, dw_hbm,
    gg_out, ug_out, xt_out, gd_out, out,
    x_full, og_full, dw, gp, up, gw, uw,
    hf, hb, hg, gg, ug, total, xt,
    rl1, rl2, rl3, rr1, rr2, rr3, asum, fa, rz,
    rb, bf, bs, bl1, bl2, bl3, br1, br2, br3,
    sib_in, mine, got, out_f,
    send, recv, local,
):
    x, zh, zl, y, c = coords()
    right, left = device(x + 1, zh, zl, y, c), device(x + 3, zh, zl, y, c)
    other, sibling = device(x, 1 - zh, zl, y, c), device(x, zh, zl, y, 1 - c)
    x1, x2, x3 = lax.rem(x + 1, 4), lax.rem(x + 2, 4), lax.rem(x + 3, 4)

    loads = [
        pltpu.make_async_copy(src, dst, local.at[i])
        for i, (src, dst) in enumerate(
            ((dw_hbm, dw), (gp_hbm, gp), (up_hbm, up), (gw_hbm, gw), (uw_hbm, uw))
        )
    ]
    for load in loads:
        load.start()
    zl_peer = [device(x, zh, 1 - zl, y + k, c) for k in range(4)]
    y_peer = [device(x, zh, zl, y + k, c) for k in (1, 2, 3)]
    partners = [right, left, other, sibling] + zl_peer + y_peer
    barrier = pltpu.get_barrier_semaphore()
    for d in partners:
        pl.semaphore_signal(barrier, inc=1, device_id=d, device_id_type=MESH)
    pl.semaphore_wait(barrier, len(partners))

    cp = Copies(send, recv)
    og = Gather(cp, 0, og_hbm, og_full, local.at[5])
    og.start_y()
    inp = Gather(cp, GATHER, x_hbm, x_full, local.at[6])
    loads[0].wait()

    @pl.loop(0, NC)
    def _(i):
        for k in range(D // 128):
            at = (pl.ds(pl.multiple_of(i * 128, 128), 128), pl.ds(k * 128, 128))
            dw[at] = dw[at] * dm[k, i].astype(F32).astype(BF)

    og.step_z()
    inp.start_y()
    og.step_y()
    og.finish()

    def partial(first, last, step):
        @pl.loop(first, last, step=step)
        def _(j):
            w = dw[pl.ds(pl.multiple_of(j * 256, 256), 256), :]
            acc = lax.dot_general(og_full[...].reshape(768, D), w, NT, preferred_element_type=F32)
            for b in range(2):
                v = acc[:, b * 128 : b * 128 + 128].reshape(2, 4, 96, 128)
                hf[2 * j + b] = v
                hb[2 * j + b] = v.astype(BF)

    B = pl.ds(NA, 6)
    BL, BR = pl.ds(0, 3), pl.ds(3, 3)
    HBL, HBR = pl.ds(NA, 3), pl.ds(NA + 3, 3)
    GA = (pl.ds(0, 2), pl.ds(2, 2))
    AL, AR = GA, (pl.ds(4, 2), pl.ds(6, 2))
    s = 2 * GATHER
    partial(4, 7, 1)
    zb = [
        cp.start(s + i, hb.at[B, 1 - zh, q], rb.at[:, q], other) for i, q in enumerate((x2, x1, x3, x))
    ]
    a1, a2 = [], []
    for g in range(2):
        partial(g, g + 3, 2)
        i = s + 4 + 6 * g
        a1.append(
            (
                cp.start(i, hb.at[AL[g], :, x2], rl1.at[GA[g]], right),
                cp.start(i + 1, hb.at[AR[g], :, x2], rr1.at[GA[g]], left),
            )
        )
        a2.append(
            (
                cp.start(i + 2, hb.at[AR[g], :, x1], rl2.at[GA[g]], right),
                cp.start(i + 3, hb.at[AL[g], :, x3], rr2.at[GA[g]], left),
            )
        )
    inp.step_z()
    loads[1].wait()
    loads[2].wait()

    def down(first, last):
        @pl.loop(first, last)
        def _(j):
            rows = pl.ds(pl.multiple_of(j * 256, 256), 256)
            gate, upv = gp[:, rows].astype(F32), up[:, rows].astype(F32)
            hidden = (gate * jax.nn.sigmoid(gate) * upv).astype(BF)
            dw[rows, :] = jnp.dot(
                hidden.T, og_full[...].reshape(768, D), preferred_element_type=F32
            ).astype(BF)

    a3 = []

    def turn_a(g):
        a1[g][0].wait_recv()
        rl1[GA[g]] = add(rl1.at[GA[g]], hf.at[AL[g], :, x1]).astype(BF)
        r = cp.start(s + 8 + 6 * g, rl1.at[GA[g]], rl3.at[GA[g]], right)
        a1[g][1].wait_recv()
        rr1[GA[g]] = add(rr1.at[GA[g]], hf.at[AR[g], :, x3]).astype(BF)
        a3.append((r, cp.start(s + 9 + 6 * g, rr1.at[GA[g]], rr3.at[GA[g]], left)))

    def land_b(i, q):
        zb[i].wait_recv()
        v = add(rb.at[:, q], hf.at[B, zh, q])
        bf[:, q] = v
        bs[:, q] = v.astype(BF)

    za = []

    def land_a(g):
        for copy in a2[g] + a3[g]:
            copy.wait_recv()
        asum[AL[g]] = add(hf.at[AL[g], :, x], rl3.at[GA[g]], rr2.at[GA[g]])
        asum[AR[g]] = add(hf.at[AR[g], :, x], rr3.at[GA[g]], rl2.at[GA[g]])
        for k, cols in enumerate((AL[g], AR[g])):
            fa[cols] = asum[cols, 1 - zh].astype(BF)
            za.append(cp.start(s + 16 + 2 * g + k, fa.at[cols], rz.at[cols], other))

    down(0, 2)
    turn_a(0)
    land_b(0, x2)
    b1r = cp.start(s + 20, bs.at[BL, x2], bl1, right)
    b1l = cp.start(s + 21, bs.at[BR, x2], br1, left)
    down(2, 3)
    turn_a(1)
    land_b(1, x1)
    b2r = cp.start(s + 22, bs.at[BR, x1], bl2, right)
    b1r.wait_recv()
    bl1[...] = add(bl1, bf.at[BL, x1]).astype(BF)
    b3r = cp.start(s + 23, bl1, bl3, right)
    down(3, 5)
    land_b(2, x3)
    b2l = cp.start(s + 24, bs.at[BL, x3], br2, left)
    b1l.wait_recv()
    br1[...] = add(br1, bf.at[BR, x3]).astype(BF)
    b3l = cp.start(s + 25, br1, br3, left)
    inp.step_y()
    land_a(0)
    land_b(3, x)
    land_a(1)
    down(5, 7)
    gd = pltpu.make_async_copy(dw, gd_out, local.at[0])
    gd.start()

    g = s + 26
    A, FL, FR = pl.ds(0, NA), pl.ds(0, 4), pl.ds(4, 4)

    def send_rows(i, cols, h, q, dev):
        piece = hg.at[cols, h, q]
        return cp.start(g + i, piece, piece, dev)

    for copy in (b2r, b2l, b3r, b3l):
        copy.wait_recv()
    hg[HBL, zh, x] = add(bf.at[BL, x], bl3, br2).astype(BF)
    hg[HBR, zh, x] = add(bf.at[BR, x], br3, bl2).astype(BF)
    br = send_rows(0, B, zh, x, right)
    bl = send_rows(1, B, zh, x, left)
    z = [send_rows(2, B, zh, x, other)]
    for copy in za:
        copy.wait_recv()
    hg[A, zh, x] = add(asum.at[:, zh], rz).astype(BF)
    ga = send_rows(3, A, zh, x, other)
    gr = [send_rows(4, A, zh, x, right)]
    gl = [send_rows(5, A, zh, x, left)]
    inp.finish()
    xt[...] = x_full[...].reshape(768, D).T
    xt_copy = pltpu.make_async_copy(xt, xt_out, local.at[5])
    xt_copy.start()
    loads[3].wait()
    mask_columns(gw, gm)
    br.wait_recv()
    fr = send_rows(6, HBL, zh, x3, right)
    z.append(send_rows(7, B, zh, x3, other))
    bl.wait_recv()
    fl = send_rows(8, HBR, zh, x1, left)
    z.append(send_rows(9, B, zh, x1, other))
    loads[4].wait()
    mask_columns(uw, um)
    gr[0].wait_recv()
    f0 = [send_rows(10, FL, zh, x3, right)]
    gl[0].wait_recv()
    f0.append(send_rows(11, FR, zh, x1, left))
    ga.wait_recv()
    gr.append(send_rows(12, A, 1 - zh, x, right))
    gl.append(send_rows(13, A, 1 - zh, x, left))
    fr.wait_recv()
    z.append(send_rows(14, HBL, zh, x2, other))
    fl.wait_recv()
    z.append(send_rows(15, HBR, zh, x2, other))

    def local_grads(h, first, last):
        rows = pl.ds(pl.multiple_of(h * 384, 128), 384)

        @pl.loop(first // 2, last // 2)
        def _(j):
            cols = pl.ds(pl.multiple_of(j * 256, 256), 256)
            gate, upv = gp[rows, cols].astype(F32), up[rows, cols].astype(F32)
            grad = jnp.concatenate(
                [hg[2 * j + b, h].reshape(384, 128).astype(F32) for b in range(2)], axis=1
            )
            sig = jax.nn.sigmoid(gate)
            gate_grad = (grad * upv * sig * (1.0 + gate * (1.0 - sig))).astype(BF)
            up_grad = (grad * gate * sig).astype(BF)
            for b in range(2):
                at = slice(b * 128, b * 128 + 128)
                gg[2 * j + b, h] = gate_grad[:, at].reshape(4, 96, 128)
                ug[2 * j + b, h] = up_grad[:, at].reshape(4, 96, 128)
            v = lax.dot_general(gate_grad, gw[:, cols], NT, preferred_element_type=F32)
            v = v + lax.dot_general(up_grad, uw[:, cols], NT, preferred_element_type=F32)
            total[h] += v.reshape(4, 2, ROWS, D)

    def write(h, i):
        copies = [
            pltpu.make_async_copy(gg.at[:, h], gg_out.at[:, h], local.at[1 + i]),
            pltpu.make_async_copy(ug.at[:, h], ug_out.at[:, h], local.at[2 + i]),
        ]
        for copy in copies:
            copy.start()
        return copies

    r = g + 18

    def to_sibling(h, i):
        return cp.start(g + 16 + i, total.at[h, :, 1 - c], sib_in.at[i], sibling)

    def piece(h, k, near, q):
        n = 4 * near + k
        return pltpu.make_async_remote_copy(
            src_ref=mine.at[h, q],
            dst_ref=got.at[n],
            send_sem=send.at[r + n],
            recv_sem=recv.at[r + n],
            device_id=device(x, zh, h, y + k, c),
            device_id_type=MESH,
        )

    def spread(h, i, copy):
        copy.wait_recv()
        mine[h] = (total[h, :, c] + sib_in[i]).astype(BF)
        near = lax.rem(h + zl, 2)

        @pl.when(near == 1)
        def _():
            piece(h, 0, near, y).start()

        for k in (1, 3, 2):
            piece(h, k, near, lax.rem(y + k, 4)).start()

    total[...] = jnp.zeros_like(total)
    local_grads(zh, 8, 14)
    for copy in f0:
        copy.wait_recv()
    local_grads(zh, 0, 8)
    near = to_sibling(zh, 0)
    writes = write(zh, 0)
    gr[1].wait_recv()
    f1 = [send_rows(18 + 8, FL, 1 - zh, x3, right)]
    gl[1].wait_recv()
    f1.append(send_rows(18 + 9, FR, 1 - zh, x1, left))
    spread(zh, 0, near)
    for copy in f1 + z:
        copy.wait_recv()
    local_grads(1 - zh, 0, 14)
    spread(1 - zh, 1, to_sibling(1 - zh, 1))
    writes += write(1 - zh, 2)
    out_f[...] = total[zl, y, c] + sib_in[lax.rem(zl + zh, 2), y]
    for n in range(1, 8):
        wait = piece(lax.rem(zl + n // 4, 2), n % 4, n // 4, y)
        wait.wait_recv()
        wait.wait_send()
        out_f[...] += got[n].astype(F32)
    out[...] = out_f[...].astype(BF)
    for copy in writes + [gd, xt_copy]:
        copy.wait()
    cp.finish()


def main(dm, gm, um, layer_input, out_grad, gate_pre, up_pre, gate_weight, up_weight, down_weight):
    vmem = pl.BlockSpec(memory_space=pltpu.VMEM)
    hbm = pl.BlockSpec(memory_space=pl.ANY)
    smem = pl.BlockSpec(memory_space=pltpu.SMEM)
    blocks = (NC, 2, 4, 96, 128)
    a = pltpu.VMEM((4, 2, 96, 128), BF)
    b = pltpu.VMEM((3, 96, 128), BF)
    copies = 2 * GATHER + 26 + 18 + 8 + 2
    return pl.pallas_call(
        main_kernel,
        name="main",
        out_shape=(
            jax.ShapeDtypeStruct(blocks, BF),
            jax.ShapeDtypeStruct(blocks, BF),
            jax.ShapeDtypeStruct((D, 768), BF),
            jax.ShapeDtypeStruct((FF, D), BF),
            jax.ShapeDtypeStruct((ROWS, D), BF),
        ),
        in_specs=[smem] * 3 + [hbm] * 7,
        out_specs=(hbm, hbm, hbm, hbm, vmem),
        scratch_shapes=[
            pltpu.VMEM((16, ROWS, D), BF),
            pltpu.VMEM((16, ROWS, D), BF),
            pltpu.VMEM((FF, D), BF),
            pltpu.VMEM((768, FF), BF),
            pltpu.VMEM((768, FF), BF),
            pltpu.VMEM((D, FF), BF),
            pltpu.VMEM((D, FF), BF),
            pltpu.VMEM(blocks, F32),
            pltpu.VMEM(blocks, BF),
            pltpu.VMEM(blocks, BF),
            pltpu.VMEM(blocks, BF),
            pltpu.VMEM(blocks, BF),
            pltpu.VMEM((2, 4, 2, ROWS, D), F32),
            pltpu.VMEM((D, 768), BF),
            a, a, a, a, a, a,
            pltpu.VMEM((NA, 2, 96, 128), F32),
            pltpu.VMEM((NA, 96, 128), BF),
            pltpu.VMEM((NA, 96, 128), BF),
            pltpu.VMEM((6, 4, 96, 128), BF),
            pltpu.VMEM((6, 4, 96, 128), F32),
            pltpu.VMEM((6, 4, 96, 128), BF),
            b, b, b, b, b, b,
            pltpu.VMEM((2, 4, ROWS, D), F32),
            pltpu.VMEM((2, 4, ROWS, D), BF),
            pltpu.VMEM((8, ROWS, D), BF),
            pltpu.VMEM((ROWS, D), F32),
            pltpu.SemaphoreType.DMA((copies,)),
            pltpu.SemaphoreType.DMA((copies,)),
            pltpu.SemaphoreType.DMA((7,)),
        ],
        compiler_params=pltpu.CompilerParams(
            collective_id=0, has_side_effects=True, vmem_limit_bytes=VMEM
        ),
    )(dm, gm, um, layer_input, out_grad, gate_pre, up_pre, gate_weight, up_weight, down_weight)


def weights_kernel(dm, gm, um, gg, ug, xt, gd, g_gate, g_up, g_down):
    j = pl.program_id(0)
    for grad, out, mask in ((gg, g_gate, gm), (ug, g_up, um)):
        rhs = jnp.concatenate([grad[0], grad[1]], axis=1)
        acc = jnp.dot(xt[...], rhs, preferred_element_type=F32)
        for a in range(D // 128):
            for b in range(2):
                at = (slice(a * 128, a * 128 + 128), slice(b * 128, b * 128 + 128))
                out[at] = (acc[at] * mask[a, 2 * j + b].astype(F32)).astype(BF)
    for a in range(2):
        for b in range(D // 128):
            at = (slice(a * 128, a * 128 + 128), slice(b * 128, b * 128 + 128))
            g_down[at] = gd[at] * dm[b, 2 * j + a].astype(F32).astype(BF)


def weights(dm, gm, um, gg, ug, xt, gd):
    smem = pl.BlockSpec(memory_space=pltpu.SMEM)
    cols = pl.BlockSpec((2, 768, 128), lambda j: (j, 0, 0))
    weight = pl.BlockSpec((D, 256), lambda j: (0, j))
    down = pl.BlockSpec((256, D), lambda j: (j, 0))
    return pl.pallas_call(
        weights_kernel,
        name="weights",
        grid=(FF // 256,),
        out_shape=(
            jax.ShapeDtypeStruct((D, FF), BF),
            jax.ShapeDtypeStruct((D, FF), BF),
            jax.ShapeDtypeStruct((FF, D), BF),
        ),
        in_specs=[smem, smem, smem, cols, cols, pl.BlockSpec((D, 768), lambda j: (0, 0)), down],
        out_specs=(weight, weight, down),
        compiler_params=pltpu.CompilerParams(vmem_limit_bytes=VMEM),
    )(dm, gm, um, gg, ug, xt, gd)


def shards(
    layer_input,
    out_grad,
    gate_pre,
    up_pre,
    gate_weight,
    up_weight,
    down_weight,
    gate_mask,
    up_mask,
    down_mask,
):
    masks = (down_mask.T, gate_mask, up_mask)
    gg, ug, xt, gd, grad_input = main(
        *masks, layer_input, out_grad, gate_pre, up_pre, gate_weight, up_weight, down_weight
    )
    grad_gate, grad_up, grad_down = weights(
        *masks, gg.reshape(NC, 768, 128), ug.reshape(NC, 768, 128), xt, gd
    )
    return (grad_input, grad_gate, grad_up, grad_down)


def solution(mesh):
    in_specs = (
        P("tensor", "pipe"),
        P("tensor", "pipe"),
        P(None, "tensor"),
        P(None, "tensor"),
        P("pipe", "tensor"),
        P("pipe", "tensor"),
        P("tensor", "pipe"),
        P("pipe", "tensor"),
        P("pipe", "tensor"),
        P("tensor", "pipe"),
    )
    out_specs = (P("tensor", "pipe"), P("pipe", "tensor"), P("pipe", "tensor"), P("tensor", "pipe"))
    return jax.shard_map(shards, mesh=mesh, in_specs=in_specs, out_specs=out_specs, check_vma=False)
```

```python
import jax
import jax.numpy as jnp
from jax import lax
from jax.experimental import pallas as pl
from jax.experimental.pallas import tpu as pltpu
from jax.sharding import PartitionSpec as P

MESH = pl.DeviceIdType.MESH
BF = jnp.bfloat16
F32 = jnp.float32
ROWS = 48
D = 1024
FF = 1792
NA = 8
NC = 14
GATHER = 15
VMEM = 63 * 1024 * 1024
PARTS = 4
COLS = D // PARTS


def coords():
    p, t = lax.axis_index("pipe"), lax.axis_index("tensor")
    return (
        lax.div(p, 2),
        lax.rem(p, 2),
        lax.div(t, 8),
        lax.rem(lax.div(t, 2), 4),
        lax.rem(t, 2),
    )


def device(x, zh, zl, y, c):
    return (lax.rem(x, 4) * 2 + zh, zl * 8 + lax.rem(y, 4) * 2 + c)


def place(zl, y, c):
    y = lax.rem(y, 4)
    return lax.rem(y, 2) * 8 + zl * 4 + lax.div(y, 2) * 2 + c


class Copies:
    def __init__(self, send, recv):
        self.send, self.recv, self.all = send, recv, []

    def start(self, i, src, dst, dev):
        c = pltpu.make_async_remote_copy(
            src_ref=src,
            dst_ref=dst,
            send_sem=self.send.at[i],
            recv_sem=self.recv.at[i],
            device_id=dev,
            device_id_type=MESH,
        )
        c.start()
        self.all.append(c)
        return c

    def finish(self):
        for c in self.all:
            c.wait_send()


class Gather:
    def __init__(self, cp, base, src, full, own):
        self.cp, self.base, self.full, self.src, self.own = cp, base, full, src, own
        x, zh, zl, y, c = self.at = coords()
        self.me = full.at[place(zl, y, c)]
        self.z = cp.start(base, src, self.me, device(x, zh, 1 - zl, y, c))
        self.n = 7
        self.y1 = [
            cp.start(base + k, src, self.me, device(x, zh, zl, y + k, c)) for k in (1, 3, 2)
        ]
        self.sib = [cp.start(base + 7, src, self.me, device(x, zh, zl, y, 1 - c))]

    def to_sibling(self, r):
        x, zh, zl, y, c = self.at
        self.n += 1
        piece = self.full.at[r]
        self.sib.append(self.cp.start(self.base + self.n, piece, piece, device(x, zh, zl, y, 1 - c)))

    def step_z(self):
        x, zh, zl, y, c = self.at
        self.z.wait_recv()
        piece = self.full.at[place(1 - zl, y, c)]
        self.y2 = [
            self.cp.start(self.base + 3 + k, piece, piece, device(x, zh, zl, y + k, c)) for k in (1, 3, 2)
        ]
        self.to_sibling(place(1 - zl, y, c))

    def step_y(self, copies, z):
        x, zh, zl, y, c = self.at
        for copy, k in zip(copies, (1, 3, 2)):
            copy.wait_recv()
            self.to_sibling(place(z, y + 4 - k, c))

    def near(self):
        self.step_y(self.y1, self.at[2])
        for copy in [self.sib[0]] + self.sib[2:]:
            copy.wait_recv()
        self.own.wait()
        self.sib = [self.sib[1]]

    def far(self):
        self.step_y(self.y2, 1 - self.at[2])
        for copy in self.sib:
            copy.wait_recv()


def add(*refs):
    total = refs[0][...].astype(F32)
    for r in refs[1:]:
        total = total + r[...].astype(F32)
    return total


def mask_columns(w, mask_ref):
    @pl.loop(0, NC)
    def _(j):
        for k in range(D // 128):
            at = (pl.ds(k * 128, 128), pl.ds(pl.multiple_of(j * 128, 128), 128))
            w[at] = w[at] * mask_ref[k, j].astype(F32).astype(BF)


NT = (((1,), (1,)), ((), ()))


def main_kernel(
    dm, gm, um, x_hbm, og_hbm, gp_hbm, up_hbm, gw_hbm, uw_hbm, dw_hbm,
    gg_out, ug_out, xt_out, gd_out, out,
    x_full, og_full, dw, gp, up, gw, uw,
    hf, hb, hg, gg, ug, by_gate, by_up, total, xt,
    rl1, rl2, rl3, rr1, rr2, rr3, asum, fa, rz,
    rb, bf, bs, bl1, bl2, bl3, br1, br2, br3,
    sib_in, mine, got,
    send, recv, local,
):
    x, zh, zl, y, c = coords()
    right, left = device(x + 1, zh, zl, y, c), device(x + 3, zh, zl, y, c)
    other, sibling = device(x, 1 - zh, zl, y, c), device(x, zh, zl, y, 1 - c)
    x1, x2, x3 = lax.rem(x + 1, 4), lax.rem(x + 2, 4), lax.rem(x + 3, 4)

    load_dw = pltpu.make_async_copy(dw_hbm, dw, local.at[0])
    load_dw.start()
    here = place(zl, y, c)
    own_og = pltpu.make_async_copy(og_hbm, og_full.at[here], local.at[1])
    own_og.start()
    own_x = pltpu.make_async_copy(x_hbm, x_full.at[here], local.at[2])
    own_x.start()
    zl_peer = [device(x, zh, 1 - zl, y + k, c) for k in range(4)]
    y_peer = [device(x, zh, zl, y + k, c) for k in (1, 2, 3)]
    partners = [right, left, other, sibling] + zl_peer + y_peer
    barrier = pltpu.get_barrier_semaphore()
    for d in partners:
        pl.semaphore_signal(barrier, inc=1, device_id=d, device_id_type=MESH)
    pl.semaphore_wait(barrier, len(partners))

    cp = Copies(send, recv)
    og = Gather(cp, 0, og_hbm, og_full, own_og)
    load_dw.wait()

    @pl.loop(0, NC)
    def _(i):
        for k in range(D // 128):
            at = (pl.ds(pl.multiple_of(i * 128, 128), 128), pl.ds(k * 128, 128))
            dw[at] = dw[at] * dm[k, i].astype(F32).astype(BF)

    og.step_z()
    inp = Gather(cp, GATHER, x_hbm, x_full, own_x)
    loads = []
    for i, (src, dst) in enumerate(((gp_hbm, gp), (up_hbm, up))):
        for h in range(2):
            loads.append(pltpu.make_async_copy(src.at[:, :, h], dst.at[h], local.at[3 + 2 * i + h]))
    for load in loads:
        load.start()

    def partial(z, first, last, step):
        @pl.loop(first, last, step=step)
        def _(j):
            w = dw[pl.ds(pl.multiple_of(j * 256, 256), 256), :]
            rows = [og_full[pl.ds(8 * h + 4 * z, 4)].reshape(192, D) for h in range(2)]
            acc = lax.dot_general(
                jnp.concatenate(rows, axis=0), w, NT, preferred_element_type=F32
            )
            for b in range(2):
                v = acc[:, b * 128 : b * 128 + 128].reshape(2, 2, 96, 128)
                hf[2 * j + b, :, pl.ds(2 * z, 2)] = v
                hb[2 * j + b, :, pl.ds(2 * z, 2)] = v.astype(BF)

    og.near()
    partial(zl, 0, 7, 1)
    og.far()

    B = pl.ds(NA, 6)
    BL, BR = pl.ds(0, 3), pl.ds(3, 3)
    HBL, HBR = pl.ds(NA, 3), pl.ds(NA + 3, 3)
    GA = (pl.ds(0, 2), pl.ds(2, 2))
    AL, AR = GA, (pl.ds(4, 2), pl.ds(6, 2))
    s = 2 * GATHER
    partial(1 - zl, 4, 7, 1)
    zb = [
        cp.start(s + i, hb.at[B, 1 - zh, q], rb.at[:, q], other) for i, q in enumerate((x2, x1, x3, x))
    ]
    a1, a2 = [], []
    for g in range(2):
        partial(1 - zl, g, g + 3, 2)
        i = s + 4 + 6 * g
        a1.append(
            (
                cp.start(i, hb.at[AL[g], :, x2], rl1.at[GA[g]], right),
                cp.start(i + 1, hb.at[AR[g], :, x2], rr1.at[GA[g]], left),
            )
        )
        a2.append(
            (
                cp.start(i + 2, hb.at[AR[g], :, x1], rl2.at[GA[g]], right),
                cp.start(i + 3, hb.at[AL[g], :, x3], rr2.at[GA[g]], left),
            )
        )
    inp.step_z()
    for load in loads:
        load.wait()
    load_gw = pltpu.make_async_copy(gw_hbm, gw, local.at[0])
    load_gw.start()
    load_uw = pltpu.make_async_copy(uw_hbm, uw, local.at[1])
    load_uw.start()

    def down(first, last):
        @pl.loop(first, last)
        def _(j):
            rows = pl.ds(pl.multiple_of(j * 256, 256), 256)
            gate = gp[..., rows].reshape(768, 256).astype(F32)
            upv = up[..., rows].reshape(768, 256).astype(F32)
            sig = jax.nn.sigmoid(gate)
            gated = gate * sig
            hidden = (gated * upv).astype(BF)
            factor = upv * sig * (1.0 + gate * (1.0 - sig))
            for b in range(2):
                at = slice(b * 128, b * 128 + 128)
                by_gate[2 * j + b] = factor[:, at].reshape(2, 4, 96, 128)
                by_up[2 * j + b] = gated[:, at].reshape(2, 4, 96, 128)
            dw[rows, :] = jnp.dot(
                hidden.T, og_full[...].reshape(768, D), preferred_element_type=F32
            ).astype(BF)

    a3 = []

    def turn_a(g):
        a1[g][0].wait_recv()
        rl1[GA[g]] = add(rl1.at[GA[g]], hf.at[AL[g], :, x1]).astype(BF)
        r = cp.start(s + 8 + 6 * g, rl1.at[GA[g]], rl3.at[GA[g]], right)
        a1[g][1].wait_recv()
        rr1[GA[g]] = add(rr1.at[GA[g]], hf.at[AR[g], :, x3]).astype(BF)
        a3.append((r, cp.start(s + 9 + 6 * g, rr1.at[GA[g]], rr3.at[GA[g]], left)))

    def land_b(i, q):
        zb[i].wait_recv()
        v = add(rb.at[:, q], hf.at[B, zh, q])
        bf[:, q] = v
        bs[:, q] = v.astype(BF)

    za = []

    def land_a(g):
        for copy in a2[g] + a3[g]:
            copy.wait_recv()
        asum[AL[g]] = add(hf.at[AL[g], :, x], rl3.at[GA[g]], rr2.at[GA[g]])
        asum[AR[g]] = add(hf.at[AR[g], :, x], rr3.at[GA[g]], rl2.at[GA[g]])
        for k, cols in enumerate((AL[g], AR[g])):
            fa[cols] = asum[cols, 1 - zh].astype(BF)
            za.append(cp.start(s + 16 + 2 * g + k, fa.at[cols], rz.at[cols], other))

    down(0, 2)
    turn_a(0)
    land_b(0, x2)
    b1r = cp.start(s + 20, bs.at[BL, x2], bl1, right)
    b1l = cp.start(s + 21, bs.at[BR, x2], br1, left)
    down(2, 3)
    turn_a(1)
    land_b(1, x1)
    b2r = cp.start(s + 22, bs.at[BR, x1], bl2, right)
    b1r.wait_recv()
    bl1[...] = add(bl1, bf.at[BL, x1]).astype(BF)
    b3r = cp.start(s + 23, bl1, bl3, right)
    down(3, 5)
    land_b(2, x3)
    b2l = cp.start(s + 24, bs.at[BL, x3], br2, left)
    b1l.wait_recv()
    br1[...] = add(br1, bf.at[BR, x3]).astype(BF)
    b3l = cp.start(s + 25, br1, br3, left)
    inp.near()
    land_a(0)
    land_b(3, x)
    land_a(1)
    down(5, 7)
    gd = pltpu.make_async_copy(dw, gd_out, local.at[3])
    gd.start()

    g = s + 26
    A, FL, FR = pl.ds(0, NA), pl.ds(0, 4), pl.ds(4, 4)

    def send_rows(i, cols, h, q, dev):
        piece = hg.at[cols, h, q]
        return cp.start(g + i, piece, piece, dev)

    for copy in (b2r, b2l, b3r, b3l):
        copy.wait_recv()
    hg[HBL, zh, x] = add(bf.at[BL, x], bl3, br2).astype(BF)
    hg[HBR, zh, x] = add(bf.at[BR, x], br3, bl2).astype(BF)
    br = send_rows(0, B, zh, x, right)
    bl = send_rows(1, B, zh, x, left)
    z = [send_rows(2, B, zh, x, other)]
    for copy in za:
        copy.wait_recv()
    hg[A, zh, x] = add(asum.at[:, zh], rz).astype(BF)
    ga = send_rows(3, A, zh, x, other)
    gr = [send_rows(4, A, zh, x, right)]
    gl = [send_rows(5, A, zh, x, left)]
    inp.far()
    xt[...] = x_full[...].reshape(768, D).T
    xt_copy = pltpu.make_async_copy(xt, xt_out, local.at[4])
    xt_copy.start()
    load_gw.wait()
    mask_columns(gw, gm)
    br.wait_recv()
    fr = send_rows(6, HBL, zh, x3, right)
    z.append(send_rows(7, B, zh, x3, other))
    bl.wait_recv()
    fl = send_rows(8, HBR, zh, x1, left)
    z.append(send_rows(9, B, zh, x1, other))
    load_uw.wait()
    mask_columns(uw, um)
    gr[0].wait_recv()
    f0 = [send_rows(10, FL, zh, x3, right)]
    gl[0].wait_recv()
    f0.append(send_rows(11, FR, zh, x1, left))
    ga.wait_recv()
    gr.append(send_rows(12, A, 1 - zh, x, right))
    gl.append(send_rows(13, A, 1 - zh, x, left))
    fr.wait_recv()
    z.append(send_rows(14, HBL, zh, x2, other))
    fl.wait_recv()
    z.append(send_rows(15, HBR, zh, x2, other))

    def local_grads(h, first, last):
        @pl.loop(first, last)
        def _(b):
            grad = hg[b, h].astype(F32)
            gg[b, h] = (grad * by_gate[b, h]).astype(BF)
            ug[b, h] = (grad * by_up[b, h]).astype(BF)

    def product(h, n, first, last):
        rows, cols = pl.ds(n * COLS, COLS), pl.ds(first * 128, (last - first) * 128)

        def half(grad, w):
            lhs = jnp.concatenate([grad[b, h].reshape(384, 128) for b in range(first, last)], axis=1)
            return lax.dot_general(lhs, w[rows, cols], NT, preferred_element_type=F32)

        return (half(gg, gw) + half(ug, uw)).reshape(4, 2, ROWS, COLS)

    def write(h, i):
        copies = [
            pltpu.make_async_copy(gg.at[:, h], gg_out.at[:, h], local.at[5 + i]),
            pltpu.make_async_copy(ug.at[:, h], ug_out.at[:, h], local.at[6 + i]),
        ]
        for copy in copies:
            copy.start()
        return copies

    t = g + 18
    r = t + 2 * PARTS

    def to_sibling(h, i, n):
        return cp.start(t + i * PARTS + n, total.at[h, n, :, 1 - c], sib_in.at[i, n], sibling)

    def piece(h, i, n, near, k):
        z, to = lax.rem(zl + k // 2, 2), y + near + 2 * (k % 2)
        q = z * 2 + lax.div(lax.rem(to, 4), 2)
        slot = 4 * near + k
        return pltpu.make_async_remote_copy(
            src_ref=mine.at[i, n, q],
            dst_ref=got.at[slot, n],
            send_sem=send.at[r + slot * PARTS + n],
            recv_sem=recv.at[r + slot * PARTS + n],
            device_id=device(x, zh, z, to, c),
            device_id_type=MESH,
        )

    def spread(h, i, n, copy):
        copy.wait_recv()
        mine[i, n] = (total[h, n, :, c] + sib_in[i, n]).astype(BF)
        near = lax.rem(h + y, 2)

        @pl.when(near == 1)
        def _():
            piece(h, i, n, near, 0).start()

        for k in (1, 2, 3):
            piece(h, i, n, near, k).start()

    local_grads(zh, 8, 14)
    for n in range(PARTS):
        total[zh, n] = product(zh, n, 8, 14)
    for copy in f0:
        copy.wait_recv()
    local_grads(zh, 0, 8)
    s0 = []
    for n in range(PARTS):
        total[zh, n] += product(zh, n, 0, 8)
        s0.append(to_sibling(zh, 0, n))
        if n == 1:
            gr[1].wait_recv()
            f1 = [send_rows(16, FL, 1 - zh, x3, right)]
            gl[1].wait_recv()
            f1.append(send_rows(17, FR, 1 - zh, x1, left))
    writes = write(zh, 0)
    for n in range(PARTS):
        spread(zh, 0, n, s0[n])
    for copy in f1 + z:
        copy.wait_recv()
    local_grads(1 - zh, 0, 14)
    writes += write(1 - zh, 2)
    s1 = []
    for n in range(PARTS):
        total[1 - zh, n] = product(1 - zh, n, 0, 14)
        s1.append(to_sibling(1 - zh, 1, n))
        if n > 0:
            spread(1 - zh, 1, n - 1, s1[n - 1])
    spread(1 - zh, 1, PARTS - 1, s1[PARTS - 1])
    own_h, own_q = lax.rem(y, 2), zl * 2 + lax.div(y, 2)
    stage = lax.rem(own_h + zh, 2)
    for n in range(PARTS):
        acc = total[own_h, n, own_q, c] + sib_in[stage, n, own_q]
        for slot in range(1, 8):
            wait = piece(0, 0, n, slot // 4, slot % 4)
            wait.wait_recv()
            wait.wait_send()
            acc = acc + got[slot, n].astype(F32)
        out[:, n * COLS : n * COLS + COLS] = acc.astype(BF)
    for copy in writes + [gd, xt_copy]:
        copy.wait()
    cp.finish()


def main(dm, gm, um, layer_input, out_grad, gate_pre, up_pre, gate_weight, up_weight, down_weight):
    vmem = pl.BlockSpec(memory_space=pltpu.VMEM)
    hbm = pl.BlockSpec(memory_space=pl.ANY)
    smem = pl.BlockSpec(memory_space=pltpu.SMEM)
    blocks = (NC, 2, 4, 96, 128)
    a = pltpu.VMEM((4, 2, 96, 128), BF)
    b = pltpu.VMEM((3, 96, 128), BF)
    copies = 2 * GATHER + 26 + 18 + 10 * PARTS
    return pl.pallas_call(
        main_kernel,
        name="main",
        out_shape=(
            jax.ShapeDtypeStruct(blocks, BF),
            jax.ShapeDtypeStruct(blocks, BF),
            jax.ShapeDtypeStruct((D, 768), BF),
            jax.ShapeDtypeStruct((FF, D), BF),
            jax.ShapeDtypeStruct((ROWS, D), BF),
        ),
        in_specs=[smem] * 3 + [hbm] * 7,
        out_specs=(hbm, hbm, hbm, hbm, vmem),
        scratch_shapes=[
            pltpu.VMEM((16, ROWS, D), BF),
            pltpu.VMEM((16, ROWS, D), BF),
            pltpu.VMEM((FF, D), BF),
            pltpu.VMEM((2, 2, 2, 96, FF), BF),
            pltpu.VMEM((2, 2, 2, 96, FF), BF),
            pltpu.VMEM((D, FF), BF),
            pltpu.VMEM((D, FF), BF),
            pltpu.VMEM(blocks, F32),
            pltpu.VMEM(blocks, BF),
            pltpu.VMEM(blocks, BF),
            pltpu.VMEM(blocks, BF),
            pltpu.VMEM(blocks, BF),
            pltpu.VMEM(blocks, F32),
            pltpu.VMEM(blocks, F32),
            pltpu.VMEM((2, PARTS, 4, 2, ROWS, COLS), F32),
            pltpu.VMEM((D, 768), BF),
            a, a, a, a, a, a,
            pltpu.VMEM((NA, 2, 96, 128), F32),
            pltpu.VMEM((NA, 96, 128), BF),
            pltpu.VMEM((NA, 96, 128), BF),
            pltpu.VMEM((6, 4, 96, 128), BF),
            pltpu.VMEM((6, 4, 96, 128), F32),
            pltpu.VMEM((6, 4, 96, 128), BF),
            b, b, b, b, b, b,
            pltpu.VMEM((2, PARTS, 4, ROWS, COLS), F32),
            pltpu.VMEM((2, PARTS, 4, ROWS, COLS), BF),
            pltpu.VMEM((8, PARTS, ROWS, COLS), BF),
            pltpu.SemaphoreType.DMA((copies,)),
            pltpu.SemaphoreType.DMA((copies,)),
            pltpu.SemaphoreType.DMA((9,)),
        ],
        compiler_params=pltpu.CompilerParams(
            collective_id=0, has_side_effects=True, vmem_limit_bytes=VMEM
        ),
    )(dm, gm, um, layer_input, out_grad, gate_pre, up_pre, gate_weight, up_weight, down_weight)


def weights_kernel(dm, gm, um, gg, ug, xt, gd, g_gate, g_up, g_down):
    j = pl.program_id(0)
    for grad, out, mask in ((gg, g_gate, gm), (ug, g_up, um)):
        rhs = jnp.concatenate([grad[0], grad[1]], axis=1)
        acc = jnp.dot(xt[...], rhs, preferred_element_type=F32)
        for a in range(D // 128):
            for b in range(2):
                at = (slice(a * 128, a * 128 + 128), slice(b * 128, b * 128 + 128))
                out[at] = (acc[at] * mask[a, 2 * j + b].astype(F32)).astype(BF)
    for a in range(2):
        for b in range(D // 128):
            at = (slice(a * 128, a * 128 + 128), slice(b * 128, b * 128 + 128))
            g_down[at] = gd[at] * dm[b, 2 * j + a].astype(F32).astype(BF)


def weights(dm, gm, um, gg, ug, xt, gd):
    smem = pl.BlockSpec(memory_space=pltpu.SMEM)
    cols = pl.BlockSpec((2, 768, 128), lambda j: (j, 0, 0))
    weight = pl.BlockSpec((D, 256), lambda j: (0, j))
    down = pl.BlockSpec((256, D), lambda j: (j, 0))
    return pl.pallas_call(
        weights_kernel,
        name="weights",
        grid=(FF // 256,),
        out_shape=(
            jax.ShapeDtypeStruct((D, FF), BF),
            jax.ShapeDtypeStruct((D, FF), BF),
            jax.ShapeDtypeStruct((FF, D), BF),
        ),
        in_specs=[smem, smem, smem, cols, cols, pl.BlockSpec((D, 768), lambda j: (0, 0)), down],
        out_specs=(weight, weight, down),
        compiler_params=pltpu.CompilerParams(vmem_limit_bytes=VMEM),
    )(dm, gm, um, gg, ug, xt, gd)


def shards(
    layer_input,
    out_grad,
    gate_pre,
    up_pre,
    gate_weight,
    up_weight,
    down_weight,
    gate_mask,
    up_mask,
    down_mask,
):
    masks = (down_mask.T, gate_mask, up_mask)
    gg, ug, xt, gd, grad_input = main(
        *masks,
        layer_input,
        out_grad,
        gate_pre.reshape(2, 2, 2, 96, FF),
        up_pre.reshape(2, 2, 2, 96, FF),
        gate_weight,
        up_weight,
        down_weight,
    )
    grad_gate, grad_up, grad_down = weights(
        *masks, gg.reshape(NC, 768, 128), ug.reshape(NC, 768, 128), xt, gd
    )
    return (grad_input, grad_gate, grad_up, grad_down)


def solution(mesh):
    in_specs = (
        P("tensor", "pipe"),
        P("tensor", "pipe"),
        P(None, "tensor"),
        P(None, "tensor"),
        P("pipe", "tensor"),
        P("pipe", "tensor"),
        P("tensor", "pipe"),
        P("pipe", "tensor"),
        P("pipe", "tensor"),
        P("tensor", "pipe"),
    )
    out_specs = (P("tensor", "pipe"), P("pipe", "tensor"), P("pipe", "tensor"), P("tensor", "pipe"))
    return jax.shard_map(shards, mesh=mesh, in_specs=in_specs, out_specs=out_specs, check_vma=False)
```

```python
import jax
import jax.numpy as jnp
from jax import lax
from jax.experimental import pallas as pl
from jax.experimental.pallas import tpu as pltpu
from jax.sharding import PartitionSpec as P

MESH = pl.DeviceIdType.MESH
BF = jnp.bfloat16
F32 = jnp.float32
ROWS = 48
D = 1024
FF = 1792
NA = 8
NC = 14
GATHER = 15
VMEM = 63 * 1024 * 1024
PARTS = 4
COLS = D // PARTS


def coords():
    p, t = lax.axis_index("pipe"), lax.axis_index("tensor")
    return (
        lax.div(p, 2),
        lax.rem(p, 2),
        lax.div(t, 8),
        lax.rem(lax.div(t, 2), 4),
        lax.rem(t, 2),
    )


def device(x, zh, zl, y, c):
    return (lax.rem(x, 4) * 2 + zh, zl * 8 + lax.rem(y, 4) * 2 + c)


def place(zl, y, c):
    y = lax.rem(y, 4)
    return lax.rem(y, 2) * 8 + zl * 4 + lax.div(y, 2) * 2 + c


class Copies:
    def __init__(self, send, recv):
        self.send, self.recv, self.all = send, recv, []

    def start(self, i, src, dst, dev):
        c = pltpu.make_async_remote_copy(
            src_ref=src,
            dst_ref=dst,
            send_sem=self.send.at[i],
            recv_sem=self.recv.at[i],
            device_id=dev,
            device_id_type=MESH,
        )
        c.start()
        self.all.append(c)
        return c

    def finish(self):
        for c in self.all:
            c.wait_send()


class Gather:
    def __init__(self, cp, base, src, full, own):
        self.cp, self.base, self.full, self.src, self.own = cp, base, full, src, own
        x, zh, zl, y, c = self.at = coords()
        self.me = full.at[place(zl, y, c)]
        own.wait()
        self.src = src = self.me
        self.z = cp.start(base, src, self.me, device(x, zh, 1 - zl, y, c))
        self.n = 7
        self.y1 = [
            cp.start(base + k, src, self.me, device(x, zh, zl, y + k, c)) for k in (1, 3, 2)
        ]
        self.sib = [cp.start(base + 7, src, self.me, device(x, zh, zl, y, 1 - c))]

    def to_sibling(self, r):
        x, zh, zl, y, c = self.at
        self.n += 1
        piece = self.full.at[r]
        self.sib.append(self.cp.start(self.base + self.n, piece, piece, device(x, zh, zl, y, 1 - c)))

    def step_z(self):
        x, zh, zl, y, c = self.at
        self.z.wait_recv()
        piece = self.full.at[place(1 - zl, y, c)]
        self.y2 = [
            self.cp.start(self.base + 3 + k, piece, piece, device(x, zh, zl, y + k, c)) for k in (1, 3, 2)
        ]
        self.to_sibling(place(1 - zl, y, c))

    def step_y(self, copies, z):
        x, zh, zl, y, c = self.at
        for copy, k in zip(copies, (1, 3, 2)):
            copy.wait_recv()
            self.to_sibling(place(z, y + 4 - k, c))

    def near(self):
        self.step_y(self.y1, self.at[2])
        for copy in [self.sib[0]] + self.sib[2:]:
            copy.wait_recv()
        self.sib = [self.sib[1]]

    def far(self):
        self.step_y(self.y2, 1 - self.at[2])
        for copy in self.sib:
            copy.wait_recv()


def add(*refs):
    total = refs[0][...].astype(F32)
    for r in refs[1:]:
        total = total + r[...].astype(F32)
    return total


def mask_columns(w, mask_ref):
    @pl.loop(0, NC)
    def _(j):
        for k in range(D // 128):
            at = (pl.ds(k * 128, 128), pl.ds(pl.multiple_of(j * 128, 128), 128))
            w[at] = w[at] * mask_ref[k, j].astype(F32).astype(BF)


NT = (((1,), (1,)), ((), ()))


def main_kernel(
    dm, gm, um, x_hbm, og_hbm, gp_hbm, up_hbm, gw_hbm, uw_hbm, dw_hbm,
    gate_out, up_out, down_out, out,
    x_full, og_full, dw, gp, up, gw, uw,
    hf, hb, hg, gg, ug, by_gate, by_up, total, xt,
    rl1, rl2, rl3, rr1, rr2, rr3, asum, fa, rz,
    rb, bf, bs, bl1, bl2, bl3, br1, br2, br3,
    sib_in, mine, got,
    send, recv, local, stored,
):
    x, zh, zl, y, c = coords()
    right, left = device(x + 1, zh, zl, y, c), device(x + 3, zh, zl, y, c)
    other, sibling = device(x, 1 - zh, zl, y, c), device(x, zh, zl, y, 1 - c)
    x1, x2, x3 = lax.rem(x + 1, 4), lax.rem(x + 2, 4), lax.rem(x + 3, 4)

    load_dw = pltpu.make_async_copy(dw_hbm, dw, local.at[0])
    load_dw.start()
    here = place(zl, y, c)
    own_og = pltpu.make_async_copy(og_hbm, og_full.at[here], local.at[1])
    own_og.start()
    own_x = pltpu.make_async_copy(x_hbm, x_full.at[here], local.at[2])
    own_x.start()
    zl_peer = [device(x, zh, 1 - zl, y + k, c) for k in range(4)]
    y_peer = [device(x, zh, zl, y + k, c) for k in (1, 2, 3)]
    partners = [right, left, other, sibling] + zl_peer + y_peer
    barrier = pltpu.get_barrier_semaphore()
    for d in partners:
        pl.semaphore_signal(barrier, inc=1, device_id=d, device_id_type=MESH)
    pl.semaphore_wait(barrier, len(partners))

    cp = Copies(send, recv)
    og = Gather(cp, 0, og_hbm, og_full, own_og)
    og.step_z()
    inp = Gather(cp, GATHER, x_hbm, x_full, own_x)
    load_dw.wait()

    @pl.loop(0, NC)
    def _(i):
        for k in range(D // 128):
            at = (pl.ds(pl.multiple_of(i * 128, 128), 128), pl.ds(k * 128, 128))
            dw[at] = dw[at] * dm[k, i].astype(F32).astype(BF)

    def partial(z, first, last, step):
        @pl.loop(first, last, step=step)
        def _(j):
            w = dw[pl.ds(pl.multiple_of(j * 256, 256), 256), :]
            rows = [og_full[pl.ds(8 * h + 4 * z, 4)].reshape(192, D) for h in range(2)]
            acc = lax.dot_general(
                jnp.concatenate(rows, axis=0), w, NT, preferred_element_type=F32
            )
            for b in range(2):
                v = acc[:, b * 128 : b * 128 + 128].reshape(2, 2, 96, 128)
                hf[2 * j + b, :, pl.ds(2 * z, 2)] = v
                hb[2 * j + b, :, pl.ds(2 * z, 2)] = v.astype(BF)

    og.near()
    partial(zl, 0, 7, 1)
    og.far()
    loads = []
    for i, (src, dst) in enumerate(((gp_hbm, gp), (up_hbm, up))):
        for h in range(2):
            loads.append(pltpu.make_async_copy(src.at[:, :, h], dst.at[h], local.at[3 + 2 * i + h]))
    for load in loads:
        load.start()

    B = pl.ds(NA, 6)
    BL, BR = pl.ds(0, 3), pl.ds(3, 3)
    HBL, HBR = pl.ds(NA, 3), pl.ds(NA + 3, 3)
    GA = (pl.ds(0, 2), pl.ds(2, 2))
    AL, AR = GA, (pl.ds(4, 2), pl.ds(6, 2))
    s = 2 * GATHER
    partial(1 - zl, 4, 7, 1)
    zb = [
        cp.start(s + i, hb.at[B, 1 - zh, q], rb.at[:, q], other) for i, q in enumerate((x2, x1, x3, x))
    ]
    a1, a2, a3, za = [], [], [], []

    def open_a(g):
        i = s + 4 + 6 * g
        a1.append(
            (
                cp.start(i, hb.at[AL[g], :, x2], rl1.at[GA[g]], right),
                cp.start(i + 1, hb.at[AR[g], :, x2], rr1.at[GA[g]], left),
            )
        )

    def direct_a(g):
        i = s + 6 + 6 * g
        a2.append(
            (
                cp.start(i, hb.at[AR[g], :, x1], rl2.at[GA[g]], right),
                cp.start(i + 1, hb.at[AL[g], :, x3], rr2.at[GA[g]], left),
            )
        )

    partial(1 - zl, 0, 3, 2)
    open_a(0)
    partial(1 - zl, 1, 4, 2)
    open_a(1)
    direct_a(0)
    inp.step_z()
    for load in loads:
        load.wait()
    load_gw = pltpu.make_async_copy(gw_hbm, gw, local.at[0])
    load_gw.start()
    load_uw = pltpu.make_async_copy(uw_hbm, uw, local.at[1])
    load_uw.start()

    def down(first, last):
        @pl.loop(first, last)
        def _(j):
            rows = pl.ds(pl.multiple_of(j * 256, 256), 256)
            gate = gp[..., rows].reshape(768, 256).astype(F32)
            upv = up[..., rows].reshape(768, 256).astype(F32)
            sig = jax.nn.sigmoid(gate)
            gated = gate * sig
            hidden = (gated * upv).astype(BF)
            factor = upv * sig * (1.0 + gate * (1.0 - sig))
            for b in range(2):
                at = slice(b * 128, b * 128 + 128)
                by_gate[2 * j + b] = factor[:, at].reshape(2, 4, 96, 128)
                by_up[2 * j + b] = gated[:, at].reshape(2, 4, 96, 128)
            acc = jnp.dot(
                hidden.T, og_full[...].reshape(768, D), preferred_element_type=F32
            ).astype(BF)
            for a in range(2):
                for b in range(D // 128):
                    keep = dm[b, 2 * j + a].astype(F32).astype(BF)
                    dw[
                        pl.ds(pl.multiple_of(j * 256 + a * 128, 128), 128), b * 128 : b * 128 + 128
                    ] = acc[a * 128 : a * 128 + 128, b * 128 : b * 128 + 128] * keep

    def turn_a(g):
        a1[g][0].wait_recv()
        rl1[GA[g]] = add(rl1.at[GA[g]], hf.at[AL[g], :, x1]).astype(BF)
        r = cp.start(s + 8 + 6 * g, rl1.at[GA[g]], rl3.at[GA[g]], right)
        a1[g][1].wait_recv()
        rr1[GA[g]] = add(rr1.at[GA[g]], hf.at[AR[g], :, x3]).astype(BF)
        a3.append((r, cp.start(s + 9 + 6 * g, rr1.at[GA[g]], rr3.at[GA[g]], left)))

    def land_b(i, q):
        zb[i].wait_recv()
        v = add(rb.at[:, q], hf.at[B, zh, q])
        bf[:, q] = v
        bs[:, q] = v.astype(BF)

    def land_a(g):
        for copy in a2[g] + a3[g]:
            copy.wait_recv()
        asum[AL[g]] = add(hf.at[AL[g], :, x], rl3.at[GA[g]], rr2.at[GA[g]])
        asum[AR[g]] = add(hf.at[AR[g], :, x], rr3.at[GA[g]], rl2.at[GA[g]])
        for k, cols in enumerate((AL[g], AR[g])):
            fa[cols] = asum[cols, 1 - zh].astype(BF)
            za.append(cp.start(s + 16 + 2 * g + k, fa.at[cols], rz.at[cols], other))

    down(0, 1)
    turn_a(0)
    land_b(0, x2)
    b1r = cp.start(s + 20, bs.at[BL, x2], bl1, right)
    b1l = cp.start(s + 21, bs.at[BR, x2], br1, left)
    turn_a(1)
    direct_a(1)
    down(1, 3)
    land_b(1, x1)
    b2r = cp.start(s + 22, bs.at[BR, x1], bl2, right)
    land_a(0)
    land_b(2, x3)
    b2l = cp.start(s + 24, bs.at[BL, x3], br2, left)
    b1r.wait_recv()
    bl1[...] = add(bl1, bf.at[BL, x1]).astype(BF)
    b3r = cp.start(s + 23, bl1, bl3, right)
    b1l.wait_recv()
    br1[...] = add(br1, bf.at[BR, x3]).astype(BF)
    b3l = cp.start(s + 25, br1, br3, left)
    inp.near()
    down(3, 5)
    land_b(3, x)
    land_a(1)
    down(5, 6)

    g = s + 26
    A, FL, FR = pl.ds(0, NA), pl.ds(0, 4), pl.ds(4, 4)

    def send_rows(i, cols, h, q, dev):
        piece = hg.at[cols, h, q]
        return cp.start(g + i, piece, piece, dev)

    for copy in (b2r, b2l, b3r, b3l):
        copy.wait_recv()
    hg[HBL, zh, x] = add(bf.at[BL, x], bl3, br2).astype(BF)
    hg[HBR, zh, x] = add(bf.at[BR, x], br3, bl2).astype(BF)
    br = send_rows(0, B, zh, x, right)
    bl = send_rows(1, B, zh, x, left)
    z = [send_rows(2, B, zh, x, other)]
    for copy in za:
        copy.wait_recv()
    hg[A, zh, x] = add(asum.at[:, zh], rz).astype(BF)
    ga = send_rows(3, A, zh, x, other)
    gr = [send_rows(4, A, zh, x, right)]
    gl = [send_rows(5, A, zh, x, left)]
    inp.far()
    down(6, 7)
    gd = pltpu.make_async_copy(dw, down_out, local.at[3])
    gd.start()
    xt[...] = x_full[...].reshape(768, D).T
    load_gw.wait()
    mask_columns(gw, gm)
    br.wait_recv()
    fr = send_rows(6, HBL, zh, x3, right)
    z.append(send_rows(7, B, zh, x3, other))
    bl.wait_recv()
    fl = send_rows(8, HBR, zh, x1, left)
    z.append(send_rows(9, B, zh, x1, other))
    load_uw.wait()
    mask_columns(uw, um)
    gr[0].wait_recv()
    f0 = [send_rows(10, FL, zh, x3, right)]
    gl[0].wait_recv()
    f0.append(send_rows(11, FR, zh, x1, left))
    ga.wait_recv()
    gr.append(send_rows(12, A, 1 - zh, x, right))
    gl.append(send_rows(13, A, 1 - zh, x, left))
    fr.wait_recv()
    z.append(send_rows(14, HBL, zh, x2, other))
    fl.wait_recv()
    z.append(send_rows(15, HBR, zh, x2, other))

    def local_grads(h, first, last):
        @pl.loop(first, last)
        def _(b):
            grad = hg[b, h].astype(F32)
            gg[b, h] = (grad * by_gate[b, h]).astype(BF)
            ug[b, h] = (grad * by_up[b, h]).astype(BF)

    def product(h, n, first, last):
        rows, cols = pl.ds(n * COLS, COLS), pl.ds(first * 128, (last - first) * 128)

        def half(grad, w):
            lhs = jnp.concatenate([grad[b, h].reshape(384, 128) for b in range(first, last)], axis=1)
            return lax.dot_general(lhs, w[rows, cols], NT, preferred_element_type=F32)

        return (half(gg, gw) + half(ug, uw)).reshape(4, 2, ROWS, COLS)

    def store(j):
        cols = pl.ds(pl.multiple_of(j * 256, 256), 256)
        return [
            pltpu.make_async_copy(gw.at[:, cols], gate_out.at[:, cols], stored.at[0, j]),
            pltpu.make_async_copy(uw.at[:, cols], up_out.at[:, cols], stored.at[1, j]),
        ]

    def weight_grads(first, last):
        @pl.loop(first, last)
        def _(j):
            for grad, w, mask in ((gg, gw, gm), (ug, uw, um)):
                rhs = jnp.concatenate([grad[2 * j + b].reshape(768, 128) for b in range(2)], axis=1)
                acc = jnp.dot(xt[...], rhs, preferred_element_type=F32).astype(BF)
                for a in range(D // 128):
                    for b in range(2):
                        keep = mask[a, 2 * j + b].astype(F32).astype(BF)
                        w[
                            a * 128 : a * 128 + 128,
                            pl.ds(pl.multiple_of(j * 256 + b * 128, 128), 128),
                        ] = acc[a * 128 : a * 128 + 128, b * 128 : b * 128 + 128] * keep
            for copy in store(j):
                copy.start()

    t = g + 18
    r = t + 2 * PARTS

    def to_sibling(h, i, n):
        return cp.start(t + i * PARTS + n, total.at[h, n, :, 1 - c], sib_in.at[i, n], sibling)

    def piece(h, i, n, near, k):
        z, to = lax.rem(zl + k // 2, 2), y + near + 2 * (k % 2)
        q = z * 2 + lax.div(lax.rem(to, 4), 2)
        slot = 4 * near + k
        return pltpu.make_async_remote_copy(
            src_ref=mine.at[i, n, q],
            dst_ref=got.at[slot, n],
            send_sem=send.at[r + slot * PARTS + n],
            recv_sem=recv.at[r + slot * PARTS + n],
            device_id=device(x, zh, z, to, c),
            device_id_type=MESH,
        )

    def spread(h, i, n, copy):
        copy.wait_recv()
        mine[i, n] = (total[h, n, :, c] + sib_in[i, n]).astype(BF)
        near = lax.rem(h + y, 2)

        @pl.when(near == 1)
        def _():
            piece(h, i, n, near, 0).start()

        for k in (1, 2, 3):
            piece(h, i, n, near, k).start()

    local_grads(zh, 8, 14)
    for n in range(PARTS):
        total[zh, n] = product(zh, n, 8, 14)
    for copy in f0:
        copy.wait_recv()
    local_grads(zh, 0, 8)
    s0 = []
    for n in range(PARTS):
        total[zh, n] += product(zh, n, 0, 8)
        s0.append(to_sibling(zh, 0, n))
    for n in range(PARTS):
        spread(zh, 0, n, s0[n])
    gr[1].wait_recv()
    f1 = [send_rows(16, FL, 1 - zh, x3, right)]
    gl[1].wait_recv()
    f1.append(send_rows(17, FR, 1 - zh, x1, left))
    for copy in f1 + z:
        copy.wait_recv()
    local_grads(1 - zh, 0, 14)
    s1 = []
    for n in range(PARTS):
        total[1 - zh, n] = product(1 - zh, n, 0, 14)
        s1.append(to_sibling(1 - zh, 1, n))
        if n > 0:
            spread(1 - zh, 1, n - 1, s1[n - 1])
    weight_grads(0, 1)
    spread(1 - zh, 1, PARTS - 1, s1[PARTS - 1])
    weight_grads(1, 7)
    own_h, own_q = lax.rem(y, 2), zl * 2 + lax.div(y, 2)
    stage = lax.rem(own_h + zh, 2)
    for n in range(PARTS):
        acc = total[own_h, n, own_q, c] + sib_in[stage, n, own_q]
        for slot in range(1, 8):
            wait = piece(0, 0, n, slot // 4, slot % 4)
            wait.wait_recv()
            wait.wait_send()
            acc = acc + got[slot, n].astype(F32)
        out[:, n * COLS : n * COLS + COLS] = acc.astype(BF)
    for j in range(7):
        for copy in store(j):
            copy.wait()
    gd.wait()
    cp.finish()


def main(dm, gm, um, layer_input, out_grad, gate_pre, up_pre, gate_weight, up_weight, down_weight):
    vmem = pl.BlockSpec(memory_space=pltpu.VMEM)
    hbm = pl.BlockSpec(memory_space=pl.ANY)
    smem = pl.BlockSpec(memory_space=pltpu.SMEM)
    blocks = (NC, 2, 4, 96, 128)
    a = pltpu.VMEM((4, 2, 96, 128), BF)
    b = pltpu.VMEM((3, 96, 128), BF)
    copies = 2 * GATHER + 26 + 18 + 10 * PARTS
    return pl.pallas_call(
        main_kernel,
        name="main",
        out_shape=(
            jax.ShapeDtypeStruct((D, FF), BF),
            jax.ShapeDtypeStruct((D, FF), BF),
            jax.ShapeDtypeStruct((FF, D), BF),
            jax.ShapeDtypeStruct((ROWS, D), BF),
        ),
        in_specs=[smem] * 3 + [hbm] * 7,
        out_specs=(hbm, hbm, hbm, vmem),
        scratch_shapes=[
            pltpu.VMEM((16, ROWS, D), BF),
            pltpu.VMEM((16, ROWS, D), BF),
            pltpu.VMEM((FF, D), BF),
            pltpu.VMEM((2, 2, 2, 96, FF), BF),
            pltpu.VMEM((2, 2, 2, 96, FF), BF),
            pltpu.VMEM((D, FF), BF),
            pltpu.VMEM((D, FF), BF),
            pltpu.VMEM(blocks, F32),
            pltpu.VMEM(blocks, BF),
            pltpu.VMEM(blocks, BF),
            pltpu.VMEM(blocks, BF),
            pltpu.VMEM(blocks, BF),
            pltpu.VMEM(blocks, F32),
            pltpu.VMEM(blocks, F32),
            pltpu.VMEM((2, PARTS, 4, 2, ROWS, COLS), F32),
            pltpu.VMEM((D, 768), BF),
            a, a, a, a, a, a,
            pltpu.VMEM((NA, 2, 96, 128), F32),
            pltpu.VMEM((NA, 96, 128), BF),
            pltpu.VMEM((NA, 96, 128), BF),
            pltpu.VMEM((6, 4, 96, 128), BF),
            pltpu.VMEM((6, 4, 96, 128), F32),
            pltpu.VMEM((6, 4, 96, 128), BF),
            b, b, b, b, b, b,
            pltpu.VMEM((2, PARTS, 4, ROWS, COLS), F32),
            pltpu.VMEM((2, PARTS, 4, ROWS, COLS), BF),
            pltpu.VMEM((8, PARTS, ROWS, COLS), BF),
            pltpu.SemaphoreType.DMA((copies,)),
            pltpu.SemaphoreType.DMA((copies,)),
            pltpu.SemaphoreType.DMA((7,)),
            pltpu.SemaphoreType.DMA((2, 7)),
        ],
        compiler_params=pltpu.CompilerParams(
            collective_id=0, has_side_effects=True, vmem_limit_bytes=VMEM
        ),
    )(dm, gm, um, layer_input, out_grad, gate_pre, up_pre, gate_weight, up_weight, down_weight)


CHUNKS = 8


def deliver_kernel(a, b, d, a_out, b_out, d_out, va, vb, vd, come, go):
    stages = []
    for k, (src, via, dst) in enumerate(((a, va, a_out), (b, vb, b_out), (d, vd, d_out))):
        rows = src.shape[0] // CHUNKS
        for i in range(CHUNKS):
            at = pl.ds(i * rows, rows)
            first = pltpu.make_async_copy(src.at[at], via.at[at], come.at[k, i])
            first.start()
            stages.append((first, pltpu.make_async_copy(via.at[at], dst.at[at], go.at[k, i])))
    for first, second in stages:
        first.wait()
        second.start()
    for _, second in stages:
        second.wait()


def deliver(*grads):
    hbm = pl.BlockSpec(memory_space=pl.ANY)
    return pl.pallas_call(
        deliver_kernel,
        name="deliver",
        out_shape=tuple(jax.ShapeDtypeStruct(g.shape, g.dtype) for g in grads),
        in_specs=[hbm] * 3,
        out_specs=(hbm,) * 3,
        scratch_shapes=[pltpu.VMEM(g.shape, g.dtype) for g in grads]
        + [pltpu.SemaphoreType.DMA((3, CHUNKS))] * 2,
        compiler_params=pltpu.CompilerParams(vmem_limit_bytes=VMEM),
    )(*grads)


def shards(
    layer_input,
    out_grad,
    gate_pre,
    up_pre,
    gate_weight,
    up_weight,
    down_weight,
    gate_mask,
    up_mask,
    down_mask,
):
    masks = (down_mask.T, gate_mask, up_mask)
    grad_gate, grad_up, grad_down, grad_input = main(
        *masks,
        layer_input,
        out_grad,
        gate_pre.reshape(2, 2, 2, 96, FF),
        up_pre.reshape(2, 2, 2, 96, FF),
        gate_weight,
        up_weight,
        down_weight,
    )
    return (grad_input, *deliver(grad_gate, grad_up, grad_down))


def solution(mesh):
    in_specs = (
        P("tensor", "pipe"),
        P("tensor", "pipe"),
        P(None, "tensor"),
        P(None, "tensor"),
        P("pipe", "tensor"),
        P("pipe", "tensor"),
        P("tensor", "pipe"),
        P("pipe", "tensor"),
        P("pipe", "tensor"),
        P("tensor", "pipe"),
    )
    out_specs = (P("tensor", "pipe"), P("pipe", "tensor"), P("pipe", "tensor"), P("tensor", "pipe"))
    return jax.shard_map(shards, mesh=mesh, in_specs=in_specs, out_specs=out_specs, check_vma=False)
```

```python
import jax
import jax.numpy as jnp
from jax import lax
from jax.experimental import pallas as pl
from jax.experimental.pallas import tpu as pltpu
from jax.sharding import PartitionSpec as P

MESH = pl.DeviceIdType.MESH
BF = jnp.bfloat16
F32 = jnp.float32
ROWS = 48
D = 1024
FF = 1792
NA = 8
NC = 14
GATHER = 15
VMEM = 63 * 1024 * 1024
PARTS = 2
COLS = D // PARTS


def coords():
    p, t = lax.axis_index("pipe"), lax.axis_index("tensor")
    return (
        lax.div(p, 2),
        lax.rem(p, 2),
        lax.div(t, 8),
        lax.rem(lax.div(t, 2), 4),
        lax.rem(t, 2),
    )


def device(x, zh, zl, y, c):
    return (lax.rem(x, 4) * 2 + zh, zl * 8 + lax.rem(y, 4) * 2 + c)


def place(zl, y, c):
    y = lax.rem(y, 4)
    return lax.rem(y, 2) * 8 + zl * 4 + lax.div(y, 2) * 2 + c


class Copies:
    def __init__(self, send, recv):
        self.send, self.recv, self.all = send, recv, []

    def start(self, i, src, dst, dev):
        c = pltpu.make_async_remote_copy(
            src_ref=src,
            dst_ref=dst,
            send_sem=self.send.at[i],
            recv_sem=self.recv.at[i],
            device_id=dev,
            device_id_type=MESH,
        )
        c.start()
        self.all.append(c)
        return c

    def finish(self):
        for c in self.all:
            c.wait_send()


class Gather:
    def __init__(self, cp, base, src, full, own):
        self.cp, self.base, self.full, self.src, self.own = cp, base, full, src, own
        x, zh, zl, y, c = self.at = coords()
        self.me = full.at[place(zl, y, c)]
        own.wait()
        self.src = src = self.me
        self.z = cp.start(base, src, self.me, device(x, zh, 1 - zl, y, c))
        self.n = 7
        self.y1 = [
            cp.start(base + k, src, self.me, device(x, zh, zl, y + k, c)) for k in (2, 1, 3)
        ]
        self.sib = [cp.start(base + 7, src, self.me, device(x, zh, zl, y, 1 - c))]

    def to_sibling(self, r):
        x, zh, zl, y, c = self.at
        self.n += 1
        piece = self.full.at[r]
        self.sib.append(self.cp.start(self.base + self.n, piece, piece, device(x, zh, zl, y, 1 - c)))

    def step_z(self):
        x, zh, zl, y, c = self.at
        self.z.wait_recv()
        piece = self.full.at[place(1 - zl, y, c)]
        self.y2 = [
            self.cp.start(self.base + 3 + k, piece, piece, device(x, zh, zl, y + k, c)) for k in (1, 3)
        ]
        self.to_sibling(place(1 - zl, y, c))

    def near(self):
        x, zh, zl, y, c = self.at
        for copy, k in zip(self.y1, (2, 1, 3)):
            copy.wait_recv()
            r = place(zl, y + 4 - k, c)
            if k == 2:
                piece = self.full.at[r]
                self.z2 = self.cp.start(self.base + 5, piece, piece, device(x, zh, 1 - zl, y, c))
            self.to_sibling(r)
        for copy in [self.sib[0]] + self.sib[2:]:
            copy.wait_recv()
        self.sib = [self.sib[1]]

    def far(self):
        x, zh, zl, y, c = self.at
        for copy, k in zip([self.z2] + self.y2, (2, 1, 3)):
            copy.wait_recv()
            self.to_sibling(place(1 - zl, y + 4 - k, c))
        for copy in self.sib:
            copy.wait_recv()


def add(*refs):
    total = refs[0][...].astype(F32)
    for r in refs[1:]:
        total = total + r[...].astype(F32)
    return total


def mask_columns(w, mask_ref):
    @pl.loop(0, NC)
    def _(j):
        for k in range(D // 128):
            at = (pl.ds(k * 128, 128), pl.ds(pl.multiple_of(j * 128, 128), 128))
            w[at] = w[at] * mask_ref[k, j].astype(F32).astype(BF)


NT = (((1,), (1,)), ((), ()))


def main_kernel(
    dm, gm, um, x_hbm, og_hbm, gp_hbm, up_hbm, gw_hbm, uw_hbm, dw_hbm,
    gate_out, up_out, down_out, out,
    x_full, og_full, dw, gp, up, gw, uw,
    hf, hb, hg, gg, ug, by_gate, by_up, total, xt,
    rl1, rl2, rl3, rr1, rr2, rr3, asum, fa, rz,
    rb, bf, bs, bl1, bl2, bl3, br1, br2, br3,
    sib_in, mine, got,
    send, recv, local, stored,
):
    x, zh, zl, y, c = coords()
    right, left = device(x + 1, zh, zl, y, c), device(x + 3, zh, zl, y, c)
    other, sibling = device(x, 1 - zh, zl, y, c), device(x, zh, zl, y, 1 - c)
    x1, x2, x3 = lax.rem(x + 1, 4), lax.rem(x + 2, 4), lax.rem(x + 3, 4)

    load_dw = pltpu.make_async_copy(dw_hbm, dw, local.at[0])
    load_dw.start()
    here = place(zl, y, c)
    own_og = pltpu.make_async_copy(og_hbm, og_full.at[here], local.at[1])
    own_og.start()
    own_x = pltpu.make_async_copy(x_hbm, x_full.at[here], local.at[2])
    own_x.start()
    zl_peer = [device(x, zh, 1 - zl, y + k, c) for k in range(4)]
    y_peer = [device(x, zh, zl, y + k, c) for k in (1, 2, 3)]
    partners = [right, left, other, sibling] + zl_peer + y_peer
    barrier = pltpu.get_barrier_semaphore()
    for d in partners:
        pl.semaphore_signal(barrier, inc=1, device_id=d, device_id_type=MESH)
    pl.semaphore_wait(barrier, len(partners))

    cp = Copies(send, recv)
    og = Gather(cp, 0, og_hbm, og_full, own_og)
    og.step_z()
    inp = Gather(cp, GATHER, x_hbm, x_full, own_x)
    load_dw.wait()

    @pl.loop(0, NC)
    def _(i):
        for k in range(D // 128):
            at = (pl.ds(pl.multiple_of(i * 128, 128), 128), pl.ds(k * 128, 128))
            dw[at] = dw[at] * dm[k, i].astype(F32).astype(BF)

    def partial(z, first, last, step):
        @pl.loop(first, last, step=step)
        def _(j):
            w = dw[pl.ds(pl.multiple_of(j * 256, 256), 256), :]
            rows = [og_full[pl.ds(8 * h + 4 * z, 4)].reshape(192, D) for h in range(2)]
            acc = lax.dot_general(
                jnp.concatenate(rows, axis=0), w, NT, preferred_element_type=F32
            )
            for b in range(2):
                v = acc[:, b * 128 : b * 128 + 128].reshape(2, 2, 96, 128)
                hf[2 * j + b, :, pl.ds(2 * z, 2)] = v
                hb[2 * j + b, :, pl.ds(2 * z, 2)] = v.astype(BF)

    og.near()
    partial(zl, 0, 7, 1)
    og.far()
    loads = []
    for i, (src, dst) in enumerate(((gp_hbm, gp), (up_hbm, up))):
        for h in range(2):
            loads.append(pltpu.make_async_copy(src.at[:, :, h], dst.at[h], local.at[3 + 2 * i + h]))
    for load in loads:
        load.start()

    B = pl.ds(NA, 6)
    BL, BR = pl.ds(0, 3), pl.ds(3, 3)
    HBL, HBR = pl.ds(NA, 3), pl.ds(NA + 3, 3)
    GA = (pl.ds(0, 2), pl.ds(2, 2))
    AL, AR = (pl.ds(0, 2), pl.ds(4, 2)), (pl.ds(2, 2), pl.ds(6, 2))
    AG = (pl.ds(0, 4), pl.ds(4, 4))
    s = 2 * GATHER
    partial(1 - zl, 4, 7, 1)
    zb = [
        cp.start(s + i, hb.at[B, 1 - zh, q], rb.at[:, q], other) for i, q in enumerate((x2, x1, x3, x))
    ]
    a1, a2, a3, za = [], [], [], []

    def open_a(g):
        i = s + 4 + 6 * g
        a1.append(
            (
                cp.start(i, hb.at[AL[g], :, x2], rl1.at[GA[g]], right),
                cp.start(i + 1, hb.at[AR[g], :, x2], rr1.at[GA[g]], left),
            )
        )

    def direct_a(g):
        i = s + 6 + 6 * g
        a2.append(
            (
                cp.start(i, hb.at[AR[g], :, x1], rl2.at[GA[g]], right),
                cp.start(i + 1, hb.at[AL[g], :, x3], rr2.at[GA[g]], left),
            )
        )

    partial(1 - zl, 0, 2, 1)
    open_a(0)
    partial(1 - zl, 2, 4, 1)
    open_a(1)
    direct_a(0)
    inp.step_z()
    for load in loads:
        load.wait()
    load_gw = pltpu.make_async_copy(gw_hbm, gw, local.at[0])
    load_gw.start()
    load_uw = pltpu.make_async_copy(uw_hbm, uw, local.at[1])
    load_uw.start()

    def down(first, last):
        @pl.loop(first, last)
        def _(j):
            rows = pl.ds(pl.multiple_of(j * 256, 256), 256)
            gate = gp[..., rows].reshape(768, 256).astype(F32)
            upv = up[..., rows].reshape(768, 256).astype(F32)
            sig = jax.nn.sigmoid(gate)
            gated = gate * sig
            hidden = (gated * upv).astype(BF)
            factor = upv * sig * (1.0 + gate * (1.0 - sig))
            for b in range(2):
                at = slice(b * 128, b * 128 + 128)
                by_gate[2 * j + b] = factor[:, at].reshape(2, 4, 96, 128)
                by_up[2 * j + b] = gated[:, at].reshape(2, 4, 96, 128)
            acc = jnp.dot(
                hidden.T, og_full[...].reshape(768, D), preferred_element_type=F32
            ).astype(BF)
            for a in range(2):
                for b in range(D // 128):
                    keep = dm[b, 2 * j + a].astype(F32).astype(BF)
                    dw[
                        pl.ds(pl.multiple_of(j * 256 + a * 128, 128), 128), b * 128 : b * 128 + 128
                    ] = acc[a * 128 : a * 128 + 128, b * 128 : b * 128 + 128] * keep

    def turn_a(g):
        a1[g][0].wait_recv()
        rl1[GA[g]] = add(rl1.at[GA[g]], hf.at[AL[g], :, x1]).astype(BF)
        r = cp.start(s + 8 + 6 * g, rl1.at[GA[g]], rl3.at[GA[g]], right)
        a1[g][1].wait_recv()
        rr1[GA[g]] = add(rr1.at[GA[g]], hf.at[AR[g], :, x3]).astype(BF)
        a3.append((r, cp.start(s + 9 + 6 * g, rr1.at[GA[g]], rr3.at[GA[g]], left)))

    def land_b(i, q):
        zb[i].wait_recv()
        v = add(rb.at[:, q], hf.at[B, zh, q])
        bf[:, q] = v
        bs[:, q] = v.astype(BF)

    def land_a(g):
        for copy in a2[g] + a3[g]:
            copy.wait_recv()
        asum[AL[g]] = add(hf.at[AL[g], :, x], rl3.at[GA[g]], rr2.at[GA[g]])
        asum[AR[g]] = add(hf.at[AR[g], :, x], rr3.at[GA[g]], rl2.at[GA[g]])
        cols = AG[g]
        fa[cols] = asum[cols, 1 - zh].astype(BF)
        za.append(cp.start(s + 16 + g, fa.at[cols], rz.at[cols], other))

    down(0, 1)
    turn_a(0)
    land_b(0, x2)
    b1r = cp.start(s + 20, bs.at[BL, x2], bl1, right)
    b1l = cp.start(s + 21, bs.at[BR, x2], br1, left)
    turn_a(1)
    direct_a(1)
    down(1, 3)
    land_b(1, x1)
    b2r = cp.start(s + 22, bs.at[BR, x1], bl2, right)
    land_a(0)
    land_b(2, x3)
    b2l = cp.start(s + 24, bs.at[BL, x3], br2, left)
    b1r.wait_recv()
    bl1[...] = add(bl1, bf.at[BL, x1]).astype(BF)
    b3r = cp.start(s + 23, bl1, bl3, right)
    b1l.wait_recv()
    br1[...] = add(br1, bf.at[BR, x3]).astype(BF)
    b3l = cp.start(s + 25, br1, br3, left)
    inp.near()
    down(3, 5)
    land_b(3, x)
    land_a(1)
    down(5, 6)

    g = s + 26
    A, FL, FR = pl.ds(0, NA), pl.ds(0, 4), pl.ds(4, 4)

    def send_rows(i, cols, h, q, dev):
        piece = hg.at[cols, h, q]
        return cp.start(g + i, piece, piece, dev)

    for copy in (b2r, b2l, b3r, b3l):
        copy.wait_recv()
    hg[HBL, zh, x] = add(bf.at[BL, x], bl3, br2).astype(BF)
    hg[HBR, zh, x] = add(bf.at[BR, x], br3, bl2).astype(BF)
    br = send_rows(0, B, zh, x, right)
    bl = send_rows(1, B, zh, x, left)
    z = [send_rows(2, B, zh, x, other)]
    for copy in za:
        copy.wait_recv()
    hg[A, zh, x] = add(asum.at[:, zh], rz).astype(BF)
    ga = send_rows(3, A, zh, x, other)
    gr = [send_rows(4, A, zh, x, right)]
    gl = [send_rows(5, A, zh, x, left)]
    inp.far()
    down(6, 7)
    gd = pltpu.make_async_copy(dw, down_out, local.at[3])
    gd.start()
    xt[...] = x_full[...].reshape(768, D).T
    load_gw.wait()
    mask_columns(gw, gm)
    br.wait_recv()
    fr = send_rows(6, HBL, zh, x3, right)
    z.append(send_rows(7, B, zh, x3, other))
    bl.wait_recv()
    fl = send_rows(8, HBR, zh, x1, left)
    z.append(send_rows(9, B, zh, x1, other))
    load_uw.wait()
    mask_columns(uw, um)
    gr[0].wait_recv()
    f0 = [send_rows(10, FL, zh, x3, right)]
    gl[0].wait_recv()
    f0.append(send_rows(11, FR, zh, x1, left))
    ga.wait_recv()
    gr.append(send_rows(12, A, 1 - zh, x, right))
    gl.append(send_rows(13, A, 1 - zh, x, left))
    fr.wait_recv()
    z.append(send_rows(14, HBL, zh, x2, other))
    fl.wait_recv()
    z.append(send_rows(15, HBR, zh, x2, other))

    def local_grads(h, q, first=0, last=NC):
        @pl.loop(first, last)
        def _(b):
            at = (b, h) if q is None else (b, h, q)
            grad = hg[at].astype(F32)
            gg[at] = (grad * by_gate[at]).astype(BF)
            ug[at] = (grad * by_up[at]).astype(BF)

    def product(h, n, first, last):
        rows, cols = pl.ds(n * COLS, COLS), pl.ds(first * 128, (last - first) * 128)

        def half(grad, w):
            lhs = jnp.concatenate([grad[b, h].reshape(384, 128) for b in range(first, last)], axis=1)
            return lax.dot_general(lhs, w[rows, cols], NT, preferred_element_type=F32)

        return (half(gg, gw) + half(ug, uw)).reshape(4, 2, ROWS, COLS)

    def store(j):
        cols = pl.ds(pl.multiple_of(j * 256, 256), 256)
        return [
            pltpu.make_async_copy(gw.at[:, cols], gate_out.at[:, cols], stored.at[0, j]),
            pltpu.make_async_copy(uw.at[:, cols], up_out.at[:, cols], stored.at[1, j]),
        ]

    def weight_grads(first, last):
        @pl.loop(first, last)
        def _(j):
            for grad, w, mask in ((gg, gw, gm), (ug, uw, um)):
                rhs = jnp.concatenate([grad[2 * j + b].reshape(768, 128) for b in range(2)], axis=1)
                acc = jnp.dot(xt[...], rhs, preferred_element_type=F32).astype(BF)
                for a in range(D // 128):
                    for b in range(2):
                        keep = mask[a, 2 * j + b].astype(F32).astype(BF)
                        w[
                            a * 128 : a * 128 + 128,
                            pl.ds(pl.multiple_of(j * 256 + b * 128, 128), 128),
                        ] = acc[a * 128 : a * 128 + 128, b * 128 : b * 128 + 128] * keep
            for copy in store(j):
                copy.start()

    t = g + 18
    r = t + 2 * PARTS

    def to_sibling(h, i, n):
        return cp.start(t + i * PARTS + n, total.at[h, n, :, 1 - c], sib_in.at[i, n], sibling)

    def piece(h, i, n, near, k):
        z, to = lax.rem(zl + k // 2, 2), y + near + 2 * (k % 2)
        q = z * 2 + lax.div(lax.rem(to, 4), 2)
        slot = 4 * near + k
        return pltpu.make_async_remote_copy(
            src_ref=mine.at[i, n, q],
            dst_ref=got.at[slot, n],
            send_sem=send.at[r + slot * PARTS + n],
            recv_sem=recv.at[r + slot * PARTS + n],
            device_id=device(x, zh, z, to, c),
            device_id_type=MESH,
        )

    def spread(h, i, n, copy):
        copy.wait_recv()
        mine[i, n] = (total[h, n, :, c] + sib_in[i, n]).astype(BF)
        near = lax.rem(h + y, 2)

        @pl.when(near == 1)
        def _():
            piece(h, i, n, near, 0).start()

        for k in (1, 2, 3):
            piece(h, i, n, near, k).start()

    local_grads(zh, None, 8, 14)
    for n in range(PARTS):
        total[zh, n] = product(zh, n, 8, 14)
    for copy in f0:
        copy.wait_recv()
    local_grads(zh, None, 0, 8)
    s0 = []
    for n in range(PARTS):
        total[zh, n] += product(zh, n, 0, 8)
        s0.append(to_sibling(zh, 0, n))
    for n in range(PARTS):
        spread(zh, 0, n, s0[n])
    gr[1].wait_recv()
    f1 = [send_rows(16, FL, 1 - zh, x3, right)]
    gl[1].wait_recv()
    f1.append(send_rows(17, FR, 1 - zh, x1, left))
    for copy in z[:3]:
        copy.wait_recv()
    for q in (x, x1, x3):
        local_grads(1 - zh, q)
    for copy in f1 + z[3:]:
        copy.wait_recv()
    local_grads(1 - zh, x2)
    s1 = []
    for n in range(PARTS):
        total[1 - zh, n] = product(1 - zh, n, 0, 14)
        s1.append(to_sibling(1 - zh, 1, n))
        if n > 0:
            spread(1 - zh, 1, n - 1, s1[n - 1])
    weight_grads(0, 1)
    spread(1 - zh, 1, PARTS - 1, s1[PARTS - 1])
    weight_grads(1, 7)
    own_h, own_q = lax.rem(y, 2), zl * 2 + lax.div(y, 2)
    stage = lax.rem(own_h + zh, 2)
    for n in range(PARTS):
        acc = total[own_h, n, own_q, c] + sib_in[stage, n, own_q]
        for slot in range(1, 8):
            wait = piece(0, 0, n, slot // 4, slot % 4)
            wait.wait_recv()
            wait.wait_send()
            acc = acc + got[slot, n].astype(F32)
        out[:, n * COLS : n * COLS + COLS] = acc.astype(BF)
    for j in range(7):
        for copy in store(j):
            copy.wait()
    gd.wait()
    cp.finish()


def main(dm, gm, um, layer_input, out_grad, gate_pre, up_pre, gate_weight, up_weight, down_weight):
    vmem = pl.BlockSpec(memory_space=pltpu.VMEM)
    hbm = pl.BlockSpec(memory_space=pl.ANY)
    smem = pl.BlockSpec(memory_space=pltpu.SMEM)
    blocks = (NC, 2, 4, 96, 128)
    a = pltpu.VMEM((4, 2, 96, 128), BF)
    b = pltpu.VMEM((3, 96, 128), BF)
    copies = 2 * GATHER + 26 + 18 + 10 * PARTS
    return pl.pallas_call(
        main_kernel,
        name="main",
        out_shape=(
            jax.ShapeDtypeStruct((D, FF), BF),
            jax.ShapeDtypeStruct((D, FF), BF),
            jax.ShapeDtypeStruct((FF, D), BF),
            jax.ShapeDtypeStruct((ROWS, D), BF),
        ),
        in_specs=[smem] * 3 + [hbm] * 7,
        out_specs=(hbm, hbm, hbm, vmem),
        scratch_shapes=[
            pltpu.VMEM((16, ROWS, D), BF),
            pltpu.VMEM((16, ROWS, D), BF),
            pltpu.VMEM((FF, D), BF),
            pltpu.VMEM((2, 2, 2, 96, FF), BF),
            pltpu.VMEM((2, 2, 2, 96, FF), BF),
            pltpu.VMEM((D, FF), BF),
            pltpu.VMEM((D, FF), BF),
            pltpu.VMEM(blocks, F32),
            pltpu.VMEM(blocks, BF),
            pltpu.VMEM(blocks, BF),
            pltpu.VMEM(blocks, BF),
            pltpu.VMEM(blocks, BF),
            pltpu.VMEM(blocks, F32),
            pltpu.VMEM(blocks, F32),
            pltpu.VMEM((2, PARTS, 4, 2, ROWS, COLS), F32),
            pltpu.VMEM((D, 768), BF),
            a, a, a, a, a, a,
            pltpu.VMEM((NA, 2, 96, 128), F32),
            pltpu.VMEM((NA, 96, 128), BF),
            pltpu.VMEM((NA, 96, 128), BF),
            pltpu.VMEM((6, 4, 96, 128), BF),
            pltpu.VMEM((6, 4, 96, 128), F32),
            pltpu.VMEM((6, 4, 96, 128), BF),
            b, b, b, b, b, b,
            pltpu.VMEM((2, PARTS, 4, ROWS, COLS), F32),
            pltpu.VMEM((2, PARTS, 4, ROWS, COLS), BF),
            pltpu.VMEM((8, PARTS, ROWS, COLS), BF),
            pltpu.SemaphoreType.DMA((copies,)),
            pltpu.SemaphoreType.DMA((copies,)),
            pltpu.SemaphoreType.DMA((7,)),
            pltpu.SemaphoreType.DMA((2, 7)),
        ],
        compiler_params=pltpu.CompilerParams(
            collective_id=0, has_side_effects=True, vmem_limit_bytes=VMEM
        ),
    )(dm, gm, um, layer_input, out_grad, gate_pre, up_pre, gate_weight, up_weight, down_weight)


CHUNKS = 8


def deliver_kernel(a, b, d, a_out, b_out, d_out, va, vb, vd, come, go):
    stages = []
    for k, (src, via, dst) in enumerate(((a, va, a_out), (b, vb, b_out), (d, vd, d_out))):
        rows = src.shape[0] // CHUNKS
        for i in range(CHUNKS):
            at = pl.ds(i * rows, rows)
            first = pltpu.make_async_copy(src.at[at], via.at[at], come.at[k, i])
            first.start()
            stages.append((first, pltpu.make_async_copy(via.at[at], dst.at[at], go.at[k, i])))
    for first, second in stages:
        first.wait()
        second.start()
    for _, second in stages:
        second.wait()


def deliver(*grads):
    hbm = pl.BlockSpec(memory_space=pl.ANY)
    return pl.pallas_call(
        deliver_kernel,
        name="deliver",
        out_shape=tuple(jax.ShapeDtypeStruct(g.shape, g.dtype) for g in grads),
        in_specs=[hbm] * 3,
        out_specs=(hbm,) * 3,
        scratch_shapes=[pltpu.VMEM(g.shape, g.dtype) for g in grads]
        + [pltpu.SemaphoreType.DMA((3, CHUNKS))] * 2,
        compiler_params=pltpu.CompilerParams(vmem_limit_bytes=VMEM),
    )(*grads)


def shards(
    layer_input,
    out_grad,
    gate_pre,
    up_pre,
    gate_weight,
    up_weight,
    down_weight,
    gate_mask,
    up_mask,
    down_mask,
):
    masks = (down_mask.T, gate_mask, up_mask)
    grad_gate, grad_up, grad_down, grad_input = main(
        *masks,
        layer_input,
        out_grad,
        gate_pre.reshape(2, 2, 2, 96, FF),
        up_pre.reshape(2, 2, 2, 96, FF),
        gate_weight,
        up_weight,
        down_weight,
    )
    return (grad_input, *deliver(grad_gate, grad_up, grad_down))


def solution(mesh):
    in_specs = (
        P("tensor", "pipe"),
        P("tensor", "pipe"),
        P(None, "tensor"),
        P(None, "tensor"),
        P("pipe", "tensor"),
        P("pipe", "tensor"),
        P("tensor", "pipe"),
        P("pipe", "tensor"),
        P("pipe", "tensor"),
        P("tensor", "pipe"),
    )
    out_specs = (P("tensor", "pipe"), P("pipe", "tensor"), P("pipe", "tensor"), P("tensor", "pipe"))
    return jax.shard_map(shards, mesh=mesh, in_specs=in_specs, out_specs=out_specs, check_vma=False)
```

```python
import jax
import jax.numpy as jnp
from jax import lax
from jax.experimental import pallas as pl
from jax.experimental.pallas import tpu as pltpu
from jax.sharding import PartitionSpec as P

MESH = pl.DeviceIdType.MESH
BF = jnp.bfloat16
F32 = jnp.float32
ROWS = 48
D = 1024
FF = 1792
NA = 8
NC = 14
GATHER = 15
VMEM = 63 * 1024 * 1024
PARTS = 2
COLS = D // PARTS


def coords():
    p, t = lax.axis_index("pipe"), lax.axis_index("tensor")
    return (
        lax.div(p, 2),
        lax.rem(p, 2),
        lax.div(t, 8),
        lax.rem(lax.div(t, 2), 4),
        lax.rem(t, 2),
    )


def device(x, zh, zl, y, c):
    return (lax.rem(x, 4) * 2 + zh, zl * 8 + lax.rem(y, 4) * 2 + c)


def place(zl, y, c):
    y = lax.rem(y, 4)
    return lax.rem(y, 2) * 8 + zl * 4 + lax.div(y, 2) * 2 + c


class Copies:
    def __init__(self, send, recv):
        self.send, self.recv, self.all = send, recv, []

    def start(self, i, src, dst, dev):
        c = pltpu.make_async_remote_copy(
            src_ref=src,
            dst_ref=dst,
            send_sem=self.send.at[i],
            recv_sem=self.recv.at[i],
            device_id=dev,
            device_id_type=MESH,
        )
        c.start()
        self.all.append(c)
        return c

    def finish(self):
        for c in self.all:
            c.wait_send()


class Gather:
    def __init__(self, cp, base, src, full, own):
        self.cp, self.base, self.full, self.src, self.own = cp, base, full, src, own
        x, zh, zl, y, c = self.at = coords()
        self.me = full.at[place(zl, y, c)]
        own.wait()
        self.src = src = self.me
        self.z = cp.start(base, src, self.me, device(x, zh, 1 - zl, y, c))
        self.n = 7
        self.y1 = [
            cp.start(base + k, src, self.me, device(x, zh, zl, y + k, c)) for k in (2, 1, 3)
        ]
        self.sib = [cp.start(base + 7, src, self.me, device(x, zh, zl, y, 1 - c))]

    def to_sibling(self, r):
        x, zh, zl, y, c = self.at
        self.n += 1
        piece = self.full.at[r]
        self.sib.append(self.cp.start(self.base + self.n, piece, piece, device(x, zh, zl, y, 1 - c)))

    def step_z(self):
        x, zh, zl, y, c = self.at
        self.z.wait_recv()
        piece = self.full.at[place(1 - zl, y, c)]
        self.y2 = [
            self.cp.start(self.base + 3 + k, piece, piece, device(x, zh, zl, y + k, c)) for k in (1, 3)
        ]
        self.to_sibling(place(1 - zl, y, c))

    def near(self):
        x, zh, zl, y, c = self.at
        for copy, k in zip(self.y1, (2, 1, 3)):
            copy.wait_recv()
            r = place(zl, y + 4 - k, c)
            if k == 2:
                piece = self.full.at[r]
                self.z2 = self.cp.start(self.base + 5, piece, piece, device(x, zh, 1 - zl, y, c))
            self.to_sibling(r)
        for copy in [self.sib[0]] + self.sib[2:]:
            copy.wait_recv()
        self.sib = [self.sib[1]]

    def far(self):
        x, zh, zl, y, c = self.at
        for copy, k in zip([self.z2] + self.y2, (2, 1, 3)):
            copy.wait_recv()
            self.to_sibling(place(1 - zl, y + 4 - k, c))
        for copy in self.sib:
            copy.wait_recv()


def add(*refs):
    total = refs[0][...].astype(F32)
    for r in refs[1:]:
        total = total + r[...].astype(F32)
    return total


def mask_columns(w, mask_ref):
    @pl.loop(0, NC)
    def _(j):
        for k in range(D // 128):
            at = (pl.ds(k * 128, 128), pl.ds(pl.multiple_of(j * 128, 128), 128))
            w[at] = w[at] * mask_ref[k, j].astype(F32).astype(BF)


NT = (((1,), (1,)), ((), ()))


def main_kernel(
    dm, gm, um, x_hbm, og_hbm, gp_hbm, up_hbm, gw_hbm, uw_hbm, dw_hbm,
    gate_out, up_out, down_out, out,
    x_full, og_full, dw, gp, up, gw, uw,
    hf, hb, hg, gg, ug, by_gate, by_up, total, xt,
    rl1, rl2, rl3, rr1, rr2, rr3, asum, fa, rz,
    rb, bf, bs, bl1, bl2, bl3, br1, br2, br3,
    sib_in, mine, got,
    send, recv, local, stored,
):
    x, zh, zl, y, c = coords()
    right, left = device(x + 1, zh, zl, y, c), device(x + 3, zh, zl, y, c)
    other, sibling = device(x, 1 - zh, zl, y, c), device(x, zh, zl, y, 1 - c)
    x1, x2, x3 = lax.rem(x + 1, 4), lax.rem(x + 2, 4), lax.rem(x + 3, 4)

    load_dw = pltpu.make_async_copy(dw_hbm, dw, local.at[0])
    load_dw.start()
    here = place(zl, y, c)
    own_og = pltpu.make_async_copy(og_hbm, og_full.at[here], local.at[1])
    own_og.start()
    own_x = pltpu.make_async_copy(x_hbm, x_full.at[here], local.at[2])
    own_x.start()
    zl_peer = [device(x, zh, 1 - zl, y + k, c) for k in range(4)]
    y_peer = [device(x, zh, zl, y + k, c) for k in (1, 2, 3)]
    partners = [right, left, other, sibling] + zl_peer + y_peer
    barrier = pltpu.get_barrier_semaphore()
    for d in partners:
        pl.semaphore_signal(barrier, inc=1, device_id=d, device_id_type=MESH)
    pl.semaphore_wait(barrier, len(partners))

    cp = Copies(send, recv)
    og = Gather(cp, 0, og_hbm, og_full, own_og)
    og.step_z()
    inp = Gather(cp, GATHER, x_hbm, x_full, own_x)
    load_dw.wait()

    @pl.loop(0, NC)
    def _(i):
        for k in range(D // 128):
            at = (pl.ds(pl.multiple_of(i * 128, 128), 128), pl.ds(k * 128, 128))
            dw[at] = dw[at] * dm[k, i].astype(F32).astype(BF)

    def partial(z, first, last, step):
        @pl.loop(first, last, step=step)
        def _(j):
            w = dw[pl.ds(pl.multiple_of(j * 256, 256), 256), :]
            rows = [og_full[pl.ds(8 * h + 4 * z, 4)].reshape(192, D) for h in range(2)]
            acc = lax.dot_general(
                jnp.concatenate(rows, axis=0), w, NT, preferred_element_type=F32
            )
            for b in range(2):
                v = acc[:, b * 128 : b * 128 + 128].reshape(2, 2, 96, 128)
                hf[2 * j + b, :, pl.ds(2 * z, 2)] = v
                hb[2 * j + b, :, pl.ds(2 * z, 2)] = v.astype(BF)

    og.near()
    partial(zl, 0, 7, 1)
    og.far()
    loads = []
    for i, (src, dst) in enumerate(((gp_hbm, gp), (up_hbm, up))):
        for h in range(2):
            loads.append(pltpu.make_async_copy(src.at[:, :, h], dst.at[h], local.at[3 + 2 * i + h]))
    for load in loads:
        load.start()

    B = pl.ds(NA, 6)
    BL, BR = pl.ds(0, 3), pl.ds(3, 3)
    HBL, HBR = pl.ds(NA, 3), pl.ds(NA + 3, 3)
    GA = (pl.ds(0, 2), pl.ds(2, 2))
    AL, AR = (pl.ds(0, 2), pl.ds(4, 2)), (pl.ds(2, 2), pl.ds(6, 2))
    AG = (pl.ds(0, 4), pl.ds(4, 4))
    s = 2 * GATHER
    partial(1 - zl, 4, 7, 1)
    zb = [
        cp.start(s + i, hb.at[B, 1 - zh, q], rb.at[:, q], other) for i, q in enumerate((x2, x1, x3, x))
    ]
    a1, a2, a3, za = [], [], [], []

    def open_a(g):
        i = s + 4 + 6 * g
        a1.append(
            (
                cp.start(i, hb.at[AL[g], :, x2], rl1.at[GA[g]], right),
                cp.start(i + 1, hb.at[AR[g], :, x2], rr1.at[GA[g]], left),
            )
        )

    def direct_a(g):
        i = s + 6 + 6 * g
        a2.append(
            (
                cp.start(i, hb.at[AR[g], :, x1], rl2.at[GA[g]], right),
                cp.start(i + 1, hb.at[AL[g], :, x3], rr2.at[GA[g]], left),
            )
        )

    partial(1 - zl, 0, 2, 1)
    open_a(0)
    partial(1 - zl, 2, 4, 1)
    open_a(1)
    direct_a(0)
    inp.step_z()
    for load in loads:
        load.wait()
    load_gw = pltpu.make_async_copy(gw_hbm, gw, local.at[0])
    load_gw.start()
    load_uw = pltpu.make_async_copy(uw_hbm, uw, local.at[1])
    load_uw.start()

    def down(first, last):
        @pl.loop(first, last)
        def _(j):
            rows = pl.ds(pl.multiple_of(j * 256, 256), 256)
            gate = gp[..., rows].reshape(768, 256).astype(F32)
            upv = up[..., rows].reshape(768, 256).astype(F32)
            sig = jax.nn.sigmoid(gate)
            gated = gate * sig
            hidden = (gated * upv).astype(BF)
            factor = upv * sig * (1.0 + gate * (1.0 - sig))
            for b in range(2):
                at = slice(b * 128, b * 128 + 128)
                by_gate[2 * j + b] = factor[:, at].reshape(2, 4, 96, 128)
                by_up[2 * j + b] = gated[:, at].reshape(2, 4, 96, 128)
            acc = jnp.dot(
                hidden.T, og_full[...].reshape(768, D), preferred_element_type=F32
            ).astype(BF)
            for a in range(2):
                for b in range(D // 128):
                    keep = dm[b, 2 * j + a].astype(F32).astype(BF)
                    dw[
                        pl.ds(pl.multiple_of(j * 256 + a * 128, 128), 128), b * 128 : b * 128 + 128
                    ] = acc[a * 128 : a * 128 + 128, b * 128 : b * 128 + 128] * keep

    def turn_a(g):
        a1[g][0].wait_recv()
        rl1[GA[g]] = add(rl1.at[GA[g]], hf.at[AL[g], :, x1]).astype(BF)
        r = cp.start(s + 8 + 6 * g, rl1.at[GA[g]], rl3.at[GA[g]], right)
        a1[g][1].wait_recv()
        rr1[GA[g]] = add(rr1.at[GA[g]], hf.at[AR[g], :, x3]).astype(BF)
        a3.append((r, cp.start(s + 9 + 6 * g, rr1.at[GA[g]], rr3.at[GA[g]], left)))

    def land_b(i, q):
        zb[i].wait_recv()
        v = add(rb.at[:, q], hf.at[B, zh, q])
        bf[:, q] = v
        bs[:, q] = v.astype(BF)

    def land_a(g):
        for copy in a2[g] + a3[g]:
            copy.wait_recv()
        asum[AL[g]] = add(hf.at[AL[g], :, x], rl3.at[GA[g]], rr2.at[GA[g]])
        asum[AR[g]] = add(hf.at[AR[g], :, x], rr3.at[GA[g]], rl2.at[GA[g]])
        cols = AG[g]
        fa[cols] = asum[cols, 1 - zh].astype(BF)
        za.append(cp.start(s + 16 + g, fa.at[cols], rz.at[cols], other))

    down(0, 1)
    turn_a(0)
    land_b(0, x2)
    b1r = cp.start(s + 20, bs.at[BL, x2], bl1, right)
    b1l = cp.start(s + 21, bs.at[BR, x2], br1, left)
    turn_a(1)
    direct_a(1)
    down(1, 3)
    land_b(1, x1)
    b2r = cp.start(s + 22, bs.at[BR, x1], bl2, right)
    land_a(0)
    land_b(2, x3)
    b2l = cp.start(s + 24, bs.at[BL, x3], br2, left)
    b1r.wait_recv()
    bl1[...] = add(bl1, bf.at[BL, x1]).astype(BF)
    b3r = cp.start(s + 23, bl1, bl3, right)
    b1l.wait_recv()
    br1[...] = add(br1, bf.at[BR, x3]).astype(BF)
    b3l = cp.start(s + 25, br1, br3, left)
    inp.near()
    down(3, 5)
    land_b(3, x)
    land_a(1)
    down(5, 6)

    g = s + 26
    A, FL, FR = pl.ds(0, NA), pl.ds(0, 4), pl.ds(4, 4)

    def send_rows(i, cols, h, q, dev):
        piece = hg.at[cols, h, q]
        return cp.start(g + i, piece, piece, dev)

    for copy in (b2r, b2l, b3r, b3l):
        copy.wait_recv()
    hg[HBL, zh, x] = add(bf.at[BL, x], bl3, br2).astype(BF)
    hg[HBR, zh, x] = add(bf.at[BR, x], br3, bl2).astype(BF)
    br = send_rows(0, B, zh, x, right)
    bl = send_rows(1, B, zh, x, left)
    z = [send_rows(2, B, zh, x, other)]
    for copy in za:
        copy.wait_recv()
    hg[A, zh, x] = add(asum.at[:, zh], rz).astype(BF)
    ga = send_rows(3, A, zh, x, other)
    gr = [send_rows(4, A, zh, x, right)]
    gl = [send_rows(5, A, zh, x, left)]
    inp.far()
    down(6, 7)
    gd = pltpu.make_async_copy(dw, down_out, local.at[3])
    gd.start()
    xt[...] = x_full[...].reshape(768, D).T
    load_gw.wait()
    mask_columns(gw, gm)
    br.wait_recv()
    fr = send_rows(6, HBL, zh, x3, right)
    z.append(send_rows(7, B, zh, x3, other))
    bl.wait_recv()
    fl = send_rows(8, HBR, zh, x1, left)
    z.append(send_rows(9, B, zh, x1, other))
    load_uw.wait()
    mask_columns(uw, um)
    gr[0].wait_recv()
    f0 = [send_rows(10, FL, zh, x3, right)]
    gl[0].wait_recv()
    f0.append(send_rows(11, FR, zh, x1, left))
    ga.wait_recv()
    gr.append(send_rows(12, A, 1 - zh, x, right))
    gl.append(send_rows(13, A, 1 - zh, x, left))
    fr.wait_recv()
    z.append(send_rows(14, HBL, zh, x2, other))
    fl.wait_recv()
    z.append(send_rows(15, HBR, zh, x2, other))

    def local_grads(h, q, first=0, last=NC):
        @pl.loop(first, last)
        def _(b):
            at = (b, h) if q is None else (b, h, q)
            grad = hg[at].astype(F32)
            gg[at] = (grad * by_gate[at]).astype(BF)
            ug[at] = (grad * by_up[at]).astype(BF)

    def product(h, n, first, last):
        rows, cols = pl.ds(n * COLS, COLS), pl.ds(first * 128, (last - first) * 128)

        def half(grad, w):
            lhs = jnp.concatenate([grad[b, h].reshape(384, 128) for b in range(first, last)], axis=1)
            return lax.dot_general(lhs, w[rows, cols], NT, preferred_element_type=F32)

        return (half(gg, gw) + half(ug, uw)).reshape(4, 2, ROWS, COLS)

    def store(j):
        cols = pl.ds(pl.multiple_of(j * 256, 256), 256)
        return [
            pltpu.make_async_copy(gw.at[:, cols], gate_out.at[:, cols], stored.at[0, j]),
            pltpu.make_async_copy(uw.at[:, cols], up_out.at[:, cols], stored.at[1, j]),
        ]

    def weight_grads(first, last):
        @pl.loop(first, last)
        def _(j):
            for grad, w, mask in ((gg, gw, gm), (ug, uw, um)):
                rhs = jnp.concatenate([grad[2 * j + b].reshape(768, 128) for b in range(2)], axis=1)
                acc = jnp.dot(xt[...], rhs, preferred_element_type=F32).astype(BF)
                for a in range(D // 128):
                    for b in range(2):
                        keep = mask[a, 2 * j + b].astype(F32).astype(BF)
                        w[
                            a * 128 : a * 128 + 128,
                            pl.ds(pl.multiple_of(j * 256 + b * 128, 128), 128),
                        ] = acc[a * 128 : a * 128 + 128, b * 128 : b * 128 + 128] * keep
            for copy in store(j):
                copy.start()

    t = g + 18
    r = t + 2 * PARTS

    def to_sibling(h, i, n):
        return cp.start(t + i * PARTS + n, total.at[h, n, :, 1 - c], sib_in.at[i, n], sibling)

    def piece(h, i, n, near, k):
        z, to = lax.rem(zl + k // 2, 2), y + near + 2 * (k % 2)
        q = z * 2 + lax.div(lax.rem(to, 4), 2)
        slot = 4 * near + k
        return pltpu.make_async_remote_copy(
            src_ref=mine.at[i, n, q],
            dst_ref=got.at[slot, n],
            send_sem=send.at[r + slot * PARTS + n],
            recv_sem=recv.at[r + slot * PARTS + n],
            device_id=device(x, zh, z, to, c),
            device_id_type=MESH,
        )

    def spread(h, i, n, copy):
        copy.wait_recv()
        mine[i, n] = (total[h, n, :, c] + sib_in[i, n]).astype(BF)
        near = lax.rem(h + y, 2)

        @pl.when(near == 1)
        def _():
            piece(h, i, n, near, 0).start()

        for k in (1, 2, 3):
            piece(h, i, n, near, k).start()

    local_grads(zh, None, 8, 14)
    for n in range(PARTS):
        total[zh, n] = product(zh, n, 8, 14)
    for copy in f0:
        copy.wait_recv()
    local_grads(zh, None, 0, 8)
    s0 = []
    for n in range(PARTS):
        total[zh, n] += product(zh, n, 0, 8)
        s0.append(to_sibling(zh, 0, n))
    gr[1].wait_recv()
    f1 = [send_rows(16, FL, 1 - zh, x3, right)]
    gl[1].wait_recv()
    f1.append(send_rows(17, FR, 1 - zh, x1, left))
    for n in range(PARTS):
        spread(zh, 0, n, s0[n])
    for copy in z[:3]:
        copy.wait_recv()
    for q in (x, x1, x3):
        local_grads(1 - zh, q)
    for copy in f1 + z[3:]:
        copy.wait_recv()
    local_grads(1 - zh, x2)
    s1 = []
    for n in range(PARTS):
        total[1 - zh, n] = product(1 - zh, n, 0, 14)
        s1.append(to_sibling(1 - zh, 1, n))
        if n > 0:
            spread(1 - zh, 1, n - 1, s1[n - 1])
    weight_grads(0, 1)
    spread(1 - zh, 1, PARTS - 1, s1[PARTS - 1])
    weight_grads(1, 7)
    own_h, own_q = lax.rem(y, 2), zl * 2 + lax.div(y, 2)
    stage = lax.rem(own_h + zh, 2)
    for n in range(PARTS):
        acc = total[own_h, n, own_q, c] + sib_in[stage, n, own_q]
        for slot in range(1, 8):
            wait = piece(0, 0, n, slot // 4, slot % 4)
            wait.wait_recv()
            wait.wait_send()
            acc = acc + got[slot, n].astype(F32)
        out[:, n * COLS : n * COLS + COLS] = acc.astype(BF)
    for j in range(7):
        for copy in store(j):
            copy.wait()
    gd.wait()
    cp.finish()


def main(dm, gm, um, layer_input, out_grad, gate_pre, up_pre, gate_weight, up_weight, down_weight):
    vmem = pl.BlockSpec(memory_space=pltpu.VMEM)
    hbm = pl.BlockSpec(memory_space=pl.ANY)
    smem = pl.BlockSpec(memory_space=pltpu.SMEM)
    blocks = (NC, 2, 4, 96, 128)
    a = pltpu.VMEM((4, 2, 96, 128), BF)
    b = pltpu.VMEM((3, 96, 128), BF)
    copies = 2 * GATHER + 26 + 18 + 10 * PARTS
    return pl.pallas_call(
        main_kernel,
        name="main",
        out_shape=(
            jax.ShapeDtypeStruct((D, FF), BF),
            jax.ShapeDtypeStruct((D, FF), BF),
            jax.ShapeDtypeStruct((FF, D), BF),
            jax.ShapeDtypeStruct((ROWS, D), BF),
        ),
        in_specs=[smem] * 3 + [hbm] * 7,
        out_specs=(hbm, hbm, hbm, vmem),
        scratch_shapes=[
            pltpu.VMEM((16, ROWS, D), BF),
            pltpu.VMEM((16, ROWS, D), BF),
            pltpu.VMEM((FF, D), BF),
            pltpu.VMEM((2, 2, 2, 96, FF), BF),
            pltpu.VMEM((2, 2, 2, 96, FF), BF),
            pltpu.VMEM((D, FF), BF),
            pltpu.VMEM((D, FF), BF),
            pltpu.VMEM(blocks, F32),
            pltpu.VMEM(blocks, BF),
            pltpu.VMEM(blocks, BF),
            pltpu.VMEM(blocks, BF),
            pltpu.VMEM(blocks, BF),
            pltpu.VMEM(blocks, F32),
            pltpu.VMEM(blocks, F32),
            pltpu.VMEM((2, PARTS, 4, 2, ROWS, COLS), F32),
            pltpu.VMEM((D, 768), BF),
            a, a, a, a, a, a,
            pltpu.VMEM((NA, 2, 96, 128), F32),
            pltpu.VMEM((NA, 96, 128), BF),
            pltpu.VMEM((NA, 96, 128), BF),
            pltpu.VMEM((6, 4, 96, 128), BF),
            pltpu.VMEM((6, 4, 96, 128), F32),
            pltpu.VMEM((6, 4, 96, 128), BF),
            b, b, b, b, b, b,
            pltpu.VMEM((2, PARTS, 4, ROWS, COLS), F32),
            pltpu.VMEM((2, PARTS, 4, ROWS, COLS), BF),
            pltpu.VMEM((8, PARTS, ROWS, COLS), BF),
            pltpu.SemaphoreType.DMA((copies,)),
            pltpu.SemaphoreType.DMA((copies,)),
            pltpu.SemaphoreType.DMA((7,)),
            pltpu.SemaphoreType.DMA((2, 7)),
        ],
        compiler_params=pltpu.CompilerParams(
            collective_id=0, has_side_effects=True, vmem_limit_bytes=VMEM
        ),
    )(dm, gm, um, layer_input, out_grad, gate_pre, up_pre, gate_weight, up_weight, down_weight)


CHUNKS = 8


def deliver_kernel(a, b, d, a_out, b_out, d_out, va, vb, vd, come, go):
    stages = []
    for k, (src, via, dst) in enumerate(((a, va, a_out), (b, vb, b_out), (d, vd, d_out))):
        rows = src.shape[0] // CHUNKS
        for i in range(CHUNKS):
            at = pl.ds(i * rows, rows)
            first = pltpu.make_async_copy(src.at[at], via.at[at], come.at[k, i])
            first.start()
            stages.append((first, pltpu.make_async_copy(via.at[at], dst.at[at], go.at[k, i])))
    for first, second in stages:
        first.wait()
        second.start()
    for _, second in stages:
        second.wait()


def deliver(*grads):
    hbm = pl.BlockSpec(memory_space=pl.ANY)
    return pl.pallas_call(
        deliver_kernel,
        name="deliver",
        out_shape=tuple(jax.ShapeDtypeStruct(g.shape, g.dtype) for g in grads),
        in_specs=[hbm] * 3,
        out_specs=(hbm,) * 3,
        scratch_shapes=[pltpu.VMEM(g.shape, g.dtype) for g in grads]
        + [pltpu.SemaphoreType.DMA((3, CHUNKS))] * 2,
        compiler_params=pltpu.CompilerParams(vmem_limit_bytes=VMEM),
    )(*grads)


def shards(
    layer_input,
    out_grad,
    gate_pre,
    up_pre,
    gate_weight,
    up_weight,
    down_weight,
    gate_mask,
    up_mask,
    down_mask,
):
    masks = (down_mask.T, gate_mask, up_mask)
    grad_gate, grad_up, grad_down, grad_input = main(
        *masks,
        layer_input,
        out_grad,
        gate_pre.reshape(2, 2, 2, 96, FF),
        up_pre.reshape(2, 2, 2, 96, FF),
        gate_weight,
        up_weight,
        down_weight,
    )
    return (grad_input, *deliver(grad_gate, grad_up, grad_down))


def solution(mesh):
    in_specs = (
        P("tensor", "pipe"),
        P("tensor", "pipe"),
        P(None, "tensor"),
        P(None, "tensor"),
        P("pipe", "tensor"),
        P("pipe", "tensor"),
        P("tensor", "pipe"),
        P("pipe", "tensor"),
        P("pipe", "tensor"),
        P("tensor", "pipe"),
    )
    out_specs = (P("tensor", "pipe"), P("pipe", "tensor"), P("pipe", "tensor"), P("tensor", "pipe"))
    return jax.shard_map(shards, mesh=mesh, in_specs=in_specs, out_specs=out_specs, check_vma=False)
```
